32 devices in a mesh: replica: 8 (over y, x, core), shard: 4 (over z).
Axes of the slice: x: 2, y: 2, z: 4, core: 2. Of those that a mesh axis runs over, the one named last changes fastest.
Arguments:
- tokens: bfloat16 [32768, 1024], P(('replica', 'shard')), may hold values from -6 to 6
- seq_start: int32 [32], P(('replica', 'shard')), may hold values from 0 to 1024, as said below
- out_grad: bfloat16 [32768, 1024], P(('replica', 'shard')), may hold values from -6 to 6
- norm_gain: bfloat16 [1024], P('shard'), may hold values from 0.099609375 to 1.8984375
- w_query: bfloat16 [1024, 512], P('shard'), may hold values from -0.1875 to 0.1875
- w_key: bfloat16 [1024, 512], P('shard'), may hold values from -0.1875 to 0.1875
- w_value: bfloat16 [1024, 1024], P('shard'), may hold values from -0.1875 to 0.1875
- w_outgate: bfloat16 [1024, 1024], P('shard'), may hold values from -0.1875 to 0.1875
- w_lowrank: bfloat16 [1024, 16], P('shard'), may hold values from -0.1875 to 0.1875
- w_rank_up: bfloat16 [16, 512], P('shard'), may hold values from -1.5 to 1.5
- gate_bias: bfloat16 [512], P('shard'), may hold values from 0 to 9
- head_gain: bfloat16 [256], P('shard'), may hold values from 0.099609375 to 1.8984375
- w_output: bfloat16 [1024, 1024], P('shard'), may hold values from -0.1875 to 0.1875
- ffn_gain: bfloat16 [1024], P('shard'), may hold values from 0.099609375 to 1.8984375
- w_gate: bfloat16 [1024, 2816], P('shard'), may hold values from -0.1875 to 0.1875
- w_up: bfloat16 [1024, 2816], P('shard'), may hold values from -0.1875 to 0.1875
- w_down: bfloat16 [2816, 1024], P('shard'), may hold values from -0.109375 to 0.109375
Outputs:
- output: bfloat16 [32768, 1024], P(('replica', 'shard'))
- tokens_grad: bfloat16 [32768, 1024], P(('replica', 'shard'))
- norm_gain_grad: float32 [1024], P('shard')
- w_query_grad: float32 [1024, 512], P('shard')
- w_key_grad: float32 [1024, 512], P('shard')
- w_value_grad: float32 [1024, 1024], P('shard')
- w_outgate_grad: float32 [1024, 1024], P('shard')
- w_lowrank_grad: float32 [1024, 16], P('shard')
- w_rank_up_grad: float32 [16, 512], P('shard')
- gate_bias_grad: float32 [512], P('shard')
- head_gain_grad: float32 [256], P('shard')
- w_output_grad: float32 [1024, 1024], P('shard')
- ffn_gain_grad: float32 [1024], P('shard')
- w_gate_grad: float32 [1024, 2816], P('shard')
- w_up_grad: float32 [1024, 2816], P('shard')
- w_down_grad: float32 [2816, 1024], P('shard')
The draws below stay inside these ranges and needn't reach their ends.
Inputs may be any that keep to these rules, and one draw needn't show every extreme that they name: `seq_start`: 1024 means that no sequence begins on the device; other values are multiples of 64; the first device holds 0; sequences begin only on devices whose index along replica+shard is a multiple of 4, and some of those devices hold no start, so that a sequence may run through several groups of 4 devices.
All inputs are finite; a program needn't handle non-finite values.
Results may differ from the reference program's by a relative error of at most 0.025.
Values may be sent and summed in bfloat16 or wider, within the bound.
A program may use at most 640 MiB of HBM per device.

```python
import jax
import jax.numpy as jnp
from jax import lax

D = 1024
HEAD_COUNT = 4
DK = 128
VALUE_WIDTH = 256
FF = 2816
RANK = 16
BLOCK = 64
SPAN = 4
TOK_DEV = 1024
KD = 512
VD = 1024
TOKENS = 32768
DEVICES = 32


def draw_seq_start(key, part):
    device_ids = jnp.arange(DEVICES, dtype=jnp.int32)
    offsets = jax.random.randint(jax.random.fold_in(key, 1), (DEVICES,), 0, TOK_DEV // BLOCK, dtype=jnp.int32) * BLOCK
    group_total = DEVICES // SPAN
    ranks = jax.random.permutation(jax.random.fold_in(key, 2), group_total).astype(jnp.int32)
    silent_groups = max(1, group_total // 4)
    silent = jnp.repeat(ranks < silent_groups, SPAN)
    starts = jnp.where(jnp.logical_and(device_ids % SPAN == 0, jnp.logical_not(silent)), offsets, TOK_DEV)
    return jnp.where(device_ids == 0, 0, starts).astype(jnp.int32)


def levels(stream_key, shape, split, smallest, high):
    def one(axis_at, blocks):
        steps = jax.random.uniform(jax.random.fold_in(jax.random.fold_in(stream_key, 6), axis_at), (blocks,), jnp.float32, smallest / len(split), high / len(split))
        return jnp.repeat(jnp.exp(steps), shape[axis_at] // blocks).reshape((-1,) + (1,) * (len(shape) - axis_at - 1))

    level = one(*split[0])
    for cut in split[1:]:
        level = level * one(*cut)
    return level


def bell_draw(rng, shape, width, reach, shards=(), kind=jnp.bfloat16):
    array = jax.random.normal(rng, shape, jnp.float32) * width
    if len(shards) > 0:
        array = levels(rng, shape, shards, -0.22, 0.18) * array
    return jnp.clip(array, min=-reach, max=reach).astype(kind)


def setup_inputs(seed: int = 0) -> dict:
    arg_keys = jax.random.split(jax.random.key(seed), 18)
    return {
        "tokens": bell_draw(arg_keys[0], (TOKENS, D), 1.0, 6.0, ((0, 32),)),
        "seq_start": draw_seq_start(jax.random.fold_in(arg_keys[17], 71), 0),
        "out_grad": bell_draw(arg_keys[2], (TOKENS, D), 1.0, 6.0, ((0, 32),)),
        "norm_gain": jnp.clip(1.0 + 0.18 * jax.random.normal(arg_keys[3], (D,), jnp.float32), 0.099609375, 1.8984375).astype(jnp.bfloat16),
        "w_query": bell_draw(arg_keys[4], (D, KD), D ** -0.5, 0.1875, ((0, 4),)),
        "w_key": bell_draw(arg_keys[5], (D, KD), D ** -0.5, 0.1875, ((0, 4),)),
        "w_value": bell_draw(arg_keys[6], (D, VD), D ** -0.5, 0.1875, ((0, 4),)),
        "w_outgate": bell_draw(arg_keys[7], (D, VD), D ** -0.5, 0.1875, ((0, 4),)),
        "w_lowrank": bell_draw(arg_keys[8], (D, RANK), D ** -0.5, 0.1875, ((0, 4),)),
        "w_rank_up": bell_draw(arg_keys[9], (RANK, KD), RANK ** -0.5, 1.5, ((0, 4),)),
        "gate_bias": jnp.clip(9.0 * jax.random.uniform(arg_keys[10], (KD,), jnp.float32) ** levels(arg_keys[10], (KD,), ((0, 4),), -0.2, 0.2), 0.0, 9.0).astype(jnp.bfloat16),
        "head_gain": jnp.clip(1.0 + 0.18 * jax.random.normal(arg_keys[11], (VALUE_WIDTH,), jnp.float32), 0.099609375, 1.8984375).astype(jnp.bfloat16),
        "w_output": bell_draw(arg_keys[12], (VD, D), VD ** -0.5, 0.1875, ((0, 4),)),
        "ffn_gain": jnp.clip(1.0 + 0.18 * jax.random.normal(arg_keys[13], (D,), jnp.float32), 0.099609375, 1.8984375).astype(jnp.bfloat16),
        "w_gate": bell_draw(arg_keys[14], (D, FF), D ** -0.5, 0.1875, ((0, 4),)),
        "w_up": bell_draw(arg_keys[15], (D, FF), D ** -0.5, 0.1875, ((0, 4),)),
        "w_down": bell_draw(arg_keys[16], (FF, D), FF ** -0.5, 0.109375, ((0, 4),)),
    }


@jax.custom_vjp
def low(v):
    return lax.optimization_barrier(v.astype(jnp.bfloat16)).astype(jnp.float32)

@jax.custom_vjp
def low_back(v):
    return v

def low_keep(v):
    return (low(v), None)

def low_pass(kept, grad):
    return (grad,)

def back_keep(v):
    return (v, None)

def back_low(kept, grad):
    return (low(grad),)
low.defvjp(low_keep, low_pass)
low_back.defvjp(back_keep, back_low)
epsilon = 1e-05
normalizer = 16.0
highest_precision = lax.Precision.HIGHEST

def product(left, right):
    return jnp.dot(left, right, precision=highest_precision, preferred_element_type=jnp.float32)

def rms_norm(values, gain):
    return values * lax.rsqrt(lax.optimization_barrier(jnp.mean(values * values, axis=-1, keepdims=True)) + epsilon) * gain

def output_gate(mixed_rows, outgate, head_gain):
    count_of_rows = mixed_rows.shape[0]
    shaped = rms_norm(mixed_rows.reshape(count_of_rows, HEAD_COUNT, VALUE_WIDTH), head_gain).reshape(count_of_rows, HEAD_COUNT * VALUE_WIDTH)
    return shaped * jax.nn.silu(outgate)

def block_step(entering_state, inputs):
    query_rows, key_rows, rows_of_value, log_decay, reset = inputs
    entering_state = entering_state * (1.0 - reset)
    cumul = jnp.cumsum(log_decay, axis=0)
    block_stop = cumul[-1]
    query_decayed = query_rows * jnp.exp(cumul)
    key_dec = key_rows * jnp.exp(-cumul)
    key_final_decay = key_rows * jnp.exp(block_stop - cumul)
    inter_block_part = jnp.einsum('gqs,qso->gqo', query_decayed, entering_state, precision=highest_precision)
    scores = jnp.einsum('ihk,jhk->hij', query_decayed, key_dec, precision=highest_precision)
    causal = jnp.tril(jnp.ones((BLOCK, BLOCK), jnp.float32))
    intra_part = jnp.einsum('hij,jhv->ihv', scores * causal, rows_of_value, precision=highest_precision)
    leaving_state = jnp.exp(block_stop)[:, :, None] * entering_state + jnp.einsum('are,aro->reo', key_final_decay, rows_of_value, precision=highest_precision)
    return (leaving_state, inter_block_part + intra_part)

def mixer(query_rows, key_rows, rows_of_value, log_decay, resets, entering_state):
    count_of_rows = query_rows.shape[0]
    block_count = count_of_rows // BLOCK
    shaped = (query_rows.reshape(block_count, BLOCK, HEAD_COUNT, DK), key_rows.reshape(block_count, BLOCK, HEAD_COUNT, DK), rows_of_value.reshape(block_count, BLOCK, HEAD_COUNT, VALUE_WIDTH), log_decay.reshape(block_count, BLOCK, HEAD_COUNT, DK), resets)
    leaving_state, mixed = lax.scan(jax.checkpoint(block_step), entering_state, shaped)
    return (mixed.reshape(count_of_rows, HEAD_COUNT * VALUE_WIDTH), leaving_state)

def layer_rows(weights, entering_state, inputs):
    norm_gain, w_query, w_key, w_value, w_outgate, w_lowrank, w_rank_up, gate_bias, head_gain, w_output, ffn_gain, w_gate, w_up, w_down = weights
    residual_in, resets = inputs
    normed = low(rms_norm(residual_in, norm_gain))
    query_rows = low_back(low(product(normed, w_query)))
    key_rows = low_back(low(product(normed, w_key)))
    rows_of_value = low_back(low(product(normed, w_value)))
    outgate = low_back(product(normed, w_outgate))
    rank_rows = low_back(low(product(normed, w_lowrank)))
    gate_logit = low_back(product(rank_rows, w_rank_up) + gate_bias)
    log_decay = jax.nn.log_sigmoid(gate_logit) / normalizer
    mixed_rows, leaving_state = mixer(query_rows, key_rows, rows_of_value, log_decay, resets, entering_state)
    gated_rows = low(output_gate(mixed_rows, outgate, head_gain))
    middle = residual_in + low_back(product(gated_rows, w_output))
    normed_ffn = low(rms_norm(middle, ffn_gain))
    gate_pre = low_back(product(normed_ffn, w_gate))
    up_pre = low_back(product(normed_ffn, w_up))
    hidden = low(jax.nn.silu(gate_pre) * up_pre)
    return (leaving_state, middle + low_back(product(hidden, w_down)))

def forward(weights, residual_all, resets):
    group_rows = 4 * TOK_DEV
    groups_count = residual_all.shape[0] // group_rows

    def step_rows(entering_state, inputs):
        return jax.checkpoint(layer_rows)(weights, entering_state, inputs)
    initial = jnp.zeros((HEAD_COUNT, DK, VALUE_WIDTH), jnp.float32)
    final, produced = lax.scan(step_rows, initial, (residual_all.reshape(groups_count, group_rows, D), resets.reshape(groups_count, group_rows // BLOCK)))
    return produced.reshape(groups_count * group_rows, D)

def reference(tokens, seq_start, out_grad, norm_gain, w_query, w_key, w_value, w_outgate, w_lowrank, w_rank_up, gate_bias, head_gain, w_output, ffn_gain, w_gate, w_up, w_down):
    weights = tuple((weight.astype(jnp.float32) for weight in (norm_gain, w_query, w_key, w_value, w_outgate, w_lowrank, w_rank_up, gate_bias, head_gain, w_output, ffn_gain, w_gate, w_up, w_down)))
    local_blocks = TOK_DEV // BLOCK
    offsets = jnp.arange(local_blocks, dtype=jnp.int32) * BLOCK
    resets = (offsets[None, :] == seq_start.astype(jnp.int32)[:, None]).astype(jnp.float32).reshape(-1)

    def whole(weight_set, residual_all):
        return forward(weight_set, residual_all, resets)
    produced, pull = jax.vjp(whole, weights, tokens.astype(jnp.float32))
    weight_grads, token_grad = pull(out_grad.astype(jnp.float32))
    return (produced.astype(jnp.bfloat16), token_grad.astype(jnp.bfloat16), weight_grads[0], weight_grads[1], weight_grads[2], weight_grads[3], weight_grads[4], weight_grads[5], weight_grads[6], weight_grads[7], weight_grads[8], weight_grads[9], weight_grads[10], weight_grads[11], weight_grads[12], weight_grads[13])
```

```python
import jax
import jax.numpy as jnp
from jax import lax
from jax.experimental import pallas as pl
from jax.experimental.pallas import tpu as pltpu
from jax.sharding import PartitionSpec as P

HEAD_COUNT = 4
DK = 128
VALUE_WIDTH = 256
BLOCK = 64
KD = HEAD_COUNT * DK
VD = HEAD_COUNT * VALUE_WIDTH
EVERY = ("replica", "shard")
ROWS = ("shard", "replica")
SIDE = 128
TAIL = 8

epsilon = 1e-05
normalizer = 16.0
highest = lax.Precision.HIGHEST
high = lax.Precision.HIGH


def dense(left, right):
    return jnp.dot(left, right, preferred_element_type=jnp.float32)


def dense_back(grad_rows, weight):
    return lax.dot_general(
        grad_rows, weight, (((1,), (1,)), ((), ())), preferred_element_type=jnp.float32
    )


def dense_left(input_rows, grad_rows):
    return lax.dot_general(
        input_rows, grad_rows, (((0,), (0,)), ((), ())), preferred_element_type=jnp.float32
    )


def rms_norm(values, gain):
    return values * lax.rsqrt(jnp.mean(values * values, axis=-1, keepdims=True) + epsilon) * gain


def output_gate(mixed_rows, outgate, head_gain):
    count_of_rows = mixed_rows.shape[0]
    shaped = rms_norm(
        mixed_rows.reshape(count_of_rows, HEAD_COUNT, VALUE_WIDTH), head_gain
    ).reshape(count_of_rows, HEAD_COUNT * VALUE_WIDTH)
    return shaped * jax.nn.silu(outgate)


def swiglu(gate_pre, up_pre):
    return jax.nn.silu(gate_pre) * up_pre


def halves(a):
    if a.dtype == jnp.bfloat16:
        return (a, None)
    top = a.astype(jnp.bfloat16)
    return (top, (a - top.astype(jnp.float32)).astype(jnp.bfloat16))


def product(left, right, dims):
    def one(a, b):
        return lax.dot_general(a, b, (dims, ((), ())), preferred_element_type=jnp.float32)

    total = one(left[0], right[0])
    if left[1] is not None:
        total = total + one(left[1], right[0])
    if right[1] is not None:
        total = total + one(left[0], right[1])
    return total


def exact(left, right):
    return lax.dot_general(
        left, right, (NT, ((), ())), precision=highest, preferred_element_type=jnp.float32
    )


NN = ((1,), (0,))
NT = ((1,), (1,))
TN = ((0,), (0,))


def causal_mask():
    rows = lax.broadcasted_iota(jnp.int32, (BLOCK, BLOCK), 0)
    cols = lax.broadcasted_iota(jnp.int32, (BLOCK, BLOCK), 1)
    return rows >= cols


def forward_kernel(start_ref, qkv_ref, cumul_ref, incoming_ref, mixed_ref, saved_ref, state_ref):
    block = pl.program_id(0)

    @pl.when(block == 0)
    def _():
        state_ref[...] = incoming_ref[...].astype(jnp.float32)

    keep = jnp.where(block * BLOCK == start_ref[0], 0.0, 1.0)
    causal = causal_mask()
    for h in range(HEAD_COUNT):
        ks = slice(h * DK, (h + 1) * DK)
        vs = slice(h * VALUE_WIDTH, (h + 1) * VALUE_WIDTH)
        query = qkv_ref[:, ks].astype(jnp.float32)
        key = qkv_ref[:, KD + h * DK : KD + (h + 1) * DK].astype(jnp.float32)
        value = qkv_ref[:, 2 * KD + h * VALUE_WIDTH : 2 * KD + (h + 1) * VALUE_WIDTH]
        cumul = cumul_ref[:, ks]
        stop = cumul[BLOCK - 1 :, :]
        state = state_ref[vs, :] * keep
        saved_ref[0, vs, :] = state
        query_f = query * jnp.exp(cumul)
        key_f = key * jnp.exp(-cumul)
        query_dec = halves(query_f)
        key_end = halves(key * jnp.exp(stop - cumul))
        scores = jnp.where(causal, exact(query_f, key_f), 0.0)
        mixed_ref[:, vs] = product(query_dec, halves(state), NT) + product(
            halves(scores), (value, None), NN
        )
        state_ref[vs, :] = state * jnp.exp(stop) + product((value, None), key_end, TN)


def backward_kernel(
    start_ref, qkv_ref, cumul_ref, grad_ref, saved_ref, outgoing_ref, gqkv_ref, gdecay_ref, back_ref
):
    step = pl.program_id(0)
    block = pl.num_programs(0) - 1 - step

    @pl.when(step == 0)
    def _():
        back_ref[...] = outgoing_ref[...].astype(jnp.float32)

    keep = jnp.where(block * BLOCK == start_ref[0], 0.0, 1.0)
    causal = causal_mask()
    suffix = jnp.where(
        lax.broadcasted_iota(jnp.int32, (BLOCK, BLOCK), 0)
        <= lax.broadcasted_iota(jnp.int32, (BLOCK, BLOCK), 1),
        1.0,
        0.0,
    )
    last = lax.broadcasted_iota(jnp.int32, (BLOCK, DK), 0) == BLOCK - 1
    for h in range(HEAD_COUNT):
        ks = slice(h * DK, (h + 1) * DK)
        ks2 = slice(KD + h * DK, KD + (h + 1) * DK)
        vs = slice(h * VALUE_WIDTH, (h + 1) * VALUE_WIDTH)
        vs2 = slice(2 * KD + h * VALUE_WIDTH, 2 * KD + (h + 1) * VALUE_WIDTH)
        query = qkv_ref[:, ks].astype(jnp.float32)
        key = qkv_ref[:, ks2].astype(jnp.float32)
        value = (qkv_ref[:, vs2], None)
        cumul = cumul_ref[:, ks]
        stop = cumul[BLOCK - 1 :, :]
        grow = jnp.exp(cumul)
        shrink = jnp.exp(-cumul)
        to_end = jnp.exp(stop - cumul)
        whole = jnp.exp(stop)
        query_f = query * grow
        key_f = key * shrink
        end_f = key * to_end
        query_dec = halves(query_f)
        key_dec = halves(key_f)
        key_end = halves(end_f)
        grad_f = grad_ref[:, vs]
        grad = halves(grad_f)
        rest = (grad_f - grad[0].astype(jnp.float32)) - grad[1].astype(jnp.float32)
        grad_value = product(grad, value, NT) + product(
            (rest.astype(jnp.bfloat16), None), value, NT
        )
        state_f = saved_ref[0, vs, :]
        back_f = back_ref[vs, :]
        state = halves(state_f)
        back = halves(back_f)
        scores = halves(jnp.where(causal, product(query_dec, key_dec, NT), 0.0))
        pull = halves(jnp.where(causal, grad_value, 0.0))
        g_query_dec = product(grad, state, NN) + product(pull, key_dec, NN)
        g_key_dec = product(pull, query_dec, TN)
        g_key_end = product(value, back, NN)
        g_value = product(scores, grad, TN) + product(key_end, back, NT)
        gqkv_ref[:, ks] = (g_query_dec * grow).astype(jnp.bfloat16)
        gqkv_ref[:, ks2] = (g_key_dec * shrink + g_key_end * to_end).astype(jnp.bfloat16)
        gqkv_ref[:, vs2] = g_value.astype(jnp.bfloat16)
        end_part = g_key_end * end_f
        at_stop = jnp.sum(end_part, axis=0, keepdims=True) + whole * jnp.sum(
            state_f * back_f, axis=0, keepdims=True
        )
        g_cumul = g_query_dec * query_f - g_key_dec * key_f - end_part
        g_cumul = g_cumul + jnp.where(last, at_stop, 0.0)
        gdecay_ref[:, ks] = lax.dot_general(
            suffix, g_cumul, (NN, ((), ())), precision=highest, preferred_element_type=jnp.float32
        )
        back_ref[vs, :] = (back_f * whole + product(grad, query_dec, TN)) * keep


def rows_spec(width, index):
    return pl.BlockSpec((BLOCK, width), index)


def mix_forward(start, qkv, cumul, incoming):
    count = qkv.shape[0] // BLOCK
    place = lambda i, s: (i, 0)
    return pl.pallas_call(
        forward_kernel,
        grid_spec=pltpu.PrefetchScalarGridSpec(
            num_scalar_prefetch=1,
            grid=(count,),
            in_specs=[
                rows_spec(2 * KD + VD, place),
                rows_spec(KD, place),
                pl.BlockSpec((VD, DK), lambda i, s: (0, 0)),
            ],
            out_specs=[
                rows_spec(VD, place),
                pl.BlockSpec((1, VD, DK), lambda i, s: (i, 0, 0)),
            ],
            scratch_shapes=[pltpu.VMEM((VD, DK), jnp.float32)],
        ),
        out_shape=[
            jax.ShapeDtypeStruct((count * BLOCK, VD), jnp.float32),
            jax.ShapeDtypeStruct((count, VD, DK), jnp.float32),
        ],
        name="mix_forward",
    )(start, qkv, cumul, incoming)


def mix_backward(start, qkv, cumul, grad, saved, outgoing):
    count = qkv.shape[0] // BLOCK
    place = lambda i, s: (count - 1 - i, 0)
    return pl.pallas_call(
        backward_kernel,
        grid_spec=pltpu.PrefetchScalarGridSpec(
            num_scalar_prefetch=1,
            grid=(count,),
            in_specs=[
                rows_spec(2 * KD + VD, place),
                rows_spec(KD, place),
                rows_spec(VD, place),
                pl.BlockSpec((1, VD, DK), lambda i, s: (count - 1 - i, 0, 0)),
                pl.BlockSpec((VD, DK), lambda i, s: (0, 0)),
            ],
            out_specs=[
                rows_spec(2 * KD + VD, place),
                rows_spec(KD, place),
            ],
            scratch_shapes=[pltpu.VMEM((VD, DK), jnp.float32)],
        ),
        out_shape=[
            jax.ShapeDtypeStruct((count * BLOCK, 2 * KD + VD), jnp.bfloat16),
            jax.ShapeDtypeStruct((count * BLOCK, KD), jnp.float32),
        ],
        name="mix_backward",
    )(start, qkv, cumul, grad, saved, outgoing)


def chain(pieces, decays, reverse):
    count = pieces.shape[0]

    def kernel(pieces_ref, decays_ref, out_ref):
        def one(step, state):
            at = count - 1 - step if reverse else step
            out_ref[at] = state.astype(jnp.bfloat16)
            return decays_ref[at] * state + pieces_ref[at].astype(jnp.float32)

        lax.fori_loop(0, count, one, jnp.zeros(pieces.shape[1:], jnp.float32))

    return pl.pallas_call(
        kernel,
        out_shape=jax.ShapeDtypeStruct(pieces.shape, jnp.bfloat16),
        name="chain_back" if reverse else "chain",
    )(pieces, decays)


def device_count():
    return lax.axis_size("replica") * lax.axis_size("shard")


def exchange_with_decay(state, decay):
    count = device_count()
    rows = VD // count
    top = decay.astype(jnp.bfloat16)
    rest = decay - top.astype(jnp.float32)
    middle = rest.astype(jnp.bfloat16)
    low = (rest - middle.astype(jnp.float32)).astype(jnp.bfloat16)
    terms = jnp.stack([top, middle, low]).reshape(3, HEAD_COUNT, DK).transpose(1, 0, 2)
    terms = jnp.pad(terms, ((0, 0), (0, TAIL - 3), (0, 0)))
    terms = jnp.repeat(terms, count // HEAD_COUNT, axis=0)
    sent = jnp.concatenate([state.astype(jnp.bfloat16).reshape(count, rows, DK), terms], axis=1)
    got = lax.all_to_all(sent, EVERY, 0, 0)
    decays = jnp.sum(got[:, rows : rows + 3].astype(jnp.float32), axis=1, keepdims=True)
    folded = chain(got[:, :rows], decays, False)
    return lax.all_to_all(folded, EVERY, 0, 0).reshape(VD, DK), decays


def exchange_back(state, decays):
    count = device_count()
    pieces = lax.all_to_all(
        state.astype(jnp.bfloat16).reshape(count, VD // count, DK), EVERY, 0, 0
    )
    folded = chain(pieces, decays, True)
    return lax.all_to_all(folded, EVERY, 0, 0).reshape(VD, DK)


def fetch(shard):
    piece = shard.shape[0] // lax.axis_size("replica")
    mine = lax.dynamic_slice_in_dim(shard, lax.axis_index("replica") * piece, piece, 0)
    return lax.all_gather(mine, ROWS, axis=0, tiled=True)


def add_low(left, right):
    return (left.astype(jnp.float32) + right.astype(jnp.float32)).astype(jnp.bfloat16)


def flip(value, bit):
    size = lax.axis_size("replica")
    return lax.ppermute(value, "replica", [(i, i ^ (1 << bit)) for i in range(size)])


def bit_of(bit):
    return (lax.axis_index("replica") >> bit) & 1


def row_bits():
    return list(range(1, lax.axis_size("replica").bit_length() - 1))


def halve(total, bits, order):
    width = total.shape[-1]
    view = total.reshape((total.shape[0],) + (2,) * len(bits) + (-1, width))
    for bit in order:
        axis = 1 + bits.index(bit)
        at = bit_of(bit)
        sent = lax.dynamic_index_in_dim(view, 1 - at, axis)
        kept = lax.dynamic_index_in_dim(view, at, axis)
        view = add_low(kept, flip(sent, bit))
    return view.reshape(total.shape[0], -1, width)


def reduce_term(left, right):
    half = right.shape[1] // 2
    at = bit_of(0)
    theirs = lax.dynamic_slice_in_dim(right, (1 - at) * half, half, 1)
    mine = lax.dynamic_slice_in_dim(right, at * half, half, 1)
    sent = dense_left(left, theirs).astype(jnp.bfloat16)
    total = add_low(dense_left(left, mine), flip(sent, 0))
    shards = lax.axis_size("shard")
    total = total.reshape(shards, -1, half)
    bits = row_bits()
    first = halve(total[: shards // 2], bits, bits)
    second = halve(total[shards // 2 :], bits, bits[::-1])
    got = lax.all_to_all(jnp.concatenate([first, second], axis=0), "shard", 0, 0)
    return jnp.sum(got.astype(jnp.float32), axis=0).astype(jnp.bfloat16)


def double(part, bits, order):
    view = part.reshape((1,) * len(bits) + part.shape)
    for bit in order:
        axis = bits.index(bit)
        got = flip(view, bit)
        view = jnp.where(
            bit_of(bit) == 0,
            jnp.concatenate([view, got], axis),
            jnp.concatenate([got, view], axis),
        )
    return view


def gather_halves(part):
    rows, width = part.shape
    bits = row_bits()
    first = double(part[: rows // 2], bits, bits)
    second = double(part[rows // 2 :], bits, bits[::-1])
    whole = jnp.concatenate([first, second], axis=len(bits)).reshape(-1, width)
    got = flip(whole, 0)
    at = bit_of(0) == 0
    return jnp.where(at, whole, got), jnp.where(at, got, whole)


def reduce_side(side):
    shards = lax.axis_size("shard")
    replicas = lax.axis_size("replica")
    width = side.shape[1]
    sent = side.astype(jnp.bfloat16).reshape(shards, replicas, -1, width).transpose(1, 0, 2, 3)
    got = lax.all_to_all(sent.reshape(shards * replicas, -1, width), EVERY, 0, 0)
    part = jnp.sum(got.astype(jnp.float32), axis=0).astype(jnp.bfloat16)
    spread = jnp.broadcast_to(part[None], (replicas,) + part.shape)
    return lax.all_to_all(spread, "replica", 0, 0).reshape(-1, width)


def column(vector, rows):
    return jnp.pad(vector, (0, rows - vector.shape[0]))[:, None]


def per_device(
    tokens,
    seq_start,
    out_grad,
    norm_gain,
    w_query,
    w_key,
    w_value,
    w_outgate,
    w_lowrank,
    w_rank_up,
    gate_bias,
    head_gain,
    w_output,
    ffn_gain,
    w_gate,
    w_up,
    w_down,
):
    shards = lax.axis_size("shard")
    rows = w_query.shape[0]
    rank = w_lowrank.shape[1]
    spread = w_rank_up.size // rows
    at_norm = rank
    at_ffn = rank + 1
    at_bias = rank + 2
    at_head = rank + 3
    at_up = rank + 4
    side = jnp.concatenate(
        [
            w_lowrank,
            norm_gain[:, None],
            ffn_gain[:, None],
            column(gate_bias, rows),
            column(head_gain, rows),
            w_rank_up.reshape(rows, spread),
            jnp.zeros((rows, SIDE - at_up - spread), jnp.bfloat16),
        ],
        axis=1,
    )
    mixer_w = fetch(jnp.concatenate([w_query, w_key, w_value, w_outgate, side], axis=1))
    output_w = fetch(w_output)
    gate_up_w = fetch(jnp.concatenate([w_gate, w_up], axis=1))
    down_w = fetch(w_down)

    qkv_width = 2 * KD + VD
    wide = qkv_width + VD
    side_w = mixer_w[:, wide:]
    lowrank_w = side_w[:, :rank]
    gain_one = side_w[:, at_norm].astype(jnp.float32)
    gain_two = side_w[:, at_ffn].astype(jnp.float32)
    bias_full = side_w[:, at_bias].reshape(shards, rows)[:, : gate_bias.shape[0]].reshape(-1)
    head_one = (
        side_w[:, at_head].reshape(shards, rows)[:, : head_gain.shape[0]].reshape(-1)
    ).astype(jnp.float32)
    rank_up_w = side_w[:, at_up : at_up + spread].reshape(rank, KD)

    residual_in = tokens.astype(jnp.float32)
    count_of_rows = residual_in.shape[0]
    block_count = count_of_rows // BLOCK
    slice_start = seq_start[0]
    normed = rms_norm(residual_in, gain_one).astype(jnp.bfloat16)
    qkv = dense(normed, mixer_w[:, :qkv_width]).astype(jnp.bfloat16)
    outgate = dense(normed, mixer_w[:, qkv_width:wide])
    rank_rows = dense(normed, lowrank_w).astype(jnp.bfloat16)
    gate_logit = dense(rank_rows, rank_up_w) + bias_full.astype(jnp.float32)
    log_decay = jax.nn.log_sigmoid(gate_logit) / normalizer

    lower = jnp.tril(jnp.ones((BLOCK, BLOCK), jnp.float32))
    cumul3 = jnp.einsum(
        "ij,bjk->bik", lower, log_decay.reshape(block_count, BLOCK, KD), precision=highest
    )
    stops = cumul3[:, -1]
    strict = jnp.tril(jnp.ones((block_count, block_count), jnp.float32), -1)
    ahead_of = jnp.dot(strict, stops, precision=highest)
    after = jnp.dot(strict.T, stops, precision=highest)
    cumul = cumul3.reshape(count_of_rows, KD)
    query_f = qkv[:, :KD].astype(jnp.float32)
    key_f = qkv[:, KD : 2 * KD].astype(jnp.float32)
    value_rows = qkv[:, 2 * KD :]
    has_start = slice_start < count_of_rows
    at = jnp.arange(count_of_rows, dtype=jnp.int32)[:, None]
    to_end = jnp.exp((stops + after)[:, None, :] - cumul3).reshape(count_of_rows, KD)
    counts = jnp.logical_or(jnp.logical_not(has_start), at >= slice_start)
    key_to_end = jnp.where(counts, key_f * to_end, 0.0)
    from_first = jnp.exp(ahead_of[:, None, :] + cumul3).reshape(count_of_rows, KD)
    query_first = jnp.where(at < slice_start, query_f * from_first, 0.0)
    carry_decay = jnp.where(has_start, 0.0, jnp.exp(jnp.sum(stops, axis=0)))

    def heads(rows_of, width):
        return rows_of.reshape(count_of_rows, HEAD_COUNT, width)

    local_end = jnp.einsum(
        "thv,thk->hvk",
        heads(value_rows.astype(jnp.float32), VALUE_WIDTH),
        heads(key_to_end, DK),
        precision=high,
    ).reshape(VD, DK)
    incoming, decays = exchange_with_decay(local_end, carry_decay)
    mixed_rows, saved = mix_forward(seq_start, qkv, cumul, incoming)
    gated_rows = output_gate(mixed_rows, outgate, head_one).astype(jnp.bfloat16)
    middle = residual_in + dense(gated_rows, output_w)
    normed_ffn = rms_norm(middle, gain_two).astype(jnp.bfloat16)
    width = w_gate.shape[1]
    gate_w = gate_up_w[:, :width]
    up_w = gate_up_w[:, width:]
    gate_pre = dense(normed_ffn, gate_w)
    up_pre = dense(normed_ffn, up_w)
    hidden = swiglu(gate_pre, up_pre).astype(jnp.bfloat16)
    output = (middle + dense(hidden, down_w)).astype(jnp.bfloat16)

    grad_out = out_grad.astype(jnp.float32)
    part_down = reduce_term(hidden, out_grad)
    grad_hidden = dense_back(out_grad, down_w)
    unused, pull_swiglu = jax.vjp(swiglu, gate_pre, up_pre)
    grad_gate_f, grad_up_f = pull_swiglu(grad_hidden)
    grad_both = jnp.concatenate(
        [grad_gate_f.astype(jnp.bfloat16), grad_up_f.astype(jnp.bfloat16)], axis=1
    )
    part_both = reduce_term(normed_ffn, grad_both)
    grad_normed_ffn = dense_back(grad_both, gate_up_w)
    unused, pull_norm_two = jax.vjp(rms_norm, middle, gain_two)
    grad_middle_part, grad_gain_two = pull_norm_two(grad_normed_ffn)
    grad_middle = grad_out + grad_middle_part
    grad_attn = grad_middle.astype(jnp.bfloat16)
    part_output = reduce_term(gated_rows, grad_attn)
    grad_gated = dense_back(grad_attn, output_w)
    unused, pull_gate = jax.vjp(output_gate, mixed_rows, outgate, head_one)
    mixed_gradient, grad_outgate_f, grad_head = pull_gate(grad_gated)
    grad_outgate = grad_outgate_f.astype(jnp.bfloat16)
    part_outgate = reduce_term(normed, grad_outgate)
    carry_grad = jnp.einsum(
        "thv,thk->hvk",
        heads(mixed_gradient, VALUE_WIDTH),
        heads(query_first, DK),
        precision=high,
    ).reshape(VD, DK)
    outgoing = exchange_back(carry_grad, decays)
    grad_qkv, grad_decay = mix_backward(
        seq_start, qkv, cumul, mixed_gradient, saved, outgoing
    )
    part_qkv = reduce_term(normed, grad_qkv)
    grad_logit = (grad_decay * jax.nn.sigmoid(-gate_logit) / normalizer).astype(jnp.bfloat16)
    grad_bias = jnp.sum(grad_logit.astype(jnp.float32), axis=0)
    grad_rank_up = dense_left(rank_rows, grad_logit)
    grad_rank = dense_back(grad_logit, rank_up_w).astype(jnp.bfloat16)
    grad_mixer = jnp.concatenate(
        [grad_qkv, grad_outgate, jnp.pad(grad_rank, ((0, 0), (0, SIDE - rank)))], axis=1
    )
    grad_normed = dense_back(grad_mixer, mixer_w)
    unused, pull_norm_one = jax.vjp(rms_norm, residual_in, gain_one)
    grad_input_part, grad_gain_one = pull_norm_one(grad_normed)
    grad_tokens = (grad_middle + grad_input_part).astype(jnp.bfloat16)

    def spread_rows(vector):
        per = vector.reshape(shards, -1)
        return jnp.pad(per, ((0, 0), (0, rows - per.shape[1]))).reshape(-1, 1)

    side_term = jnp.concatenate(
        [
            dense_left(normed, grad_rank),
            grad_gain_one[:, None],
            grad_gain_two[:, None],
            spread_rows(grad_bias),
            spread_rows(grad_head),
            grad_rank_up.reshape(shards * rows, spread),
            jnp.zeros((shards * rows, SIDE - at_up - spread), jnp.float32),
        ],
        axis=1,
    )
    side_sum = reduce_side(side_term).astype(jnp.float32)

    def final(part):
        return tuple(half.astype(jnp.float32) for half in gather_halves(part))

    def joined(part):
        return jnp.concatenate(final(part), axis=1)

    sum_down = joined(part_down)
    sum_gate, sum_up = final(part_both)
    sum_output = joined(part_output)
    sum_outgate = joined(part_outgate)
    query_key, sum_value = final(part_qkv)
    return (
        output,
        grad_tokens,
        side_sum[:, at_norm],
        query_key[:, :KD],
        query_key[:, KD:],
        sum_value,
        sum_outgate,
        side_sum[:, :rank],
        side_sum[:, at_up : at_up + spread].reshape(w_rank_up.shape),
        side_sum[: gate_bias.shape[0], at_bias],
        side_sum[: head_gain.shape[0], at_head],
        sum_output,
        side_sum[:, at_ffn],
        sum_gate,
        sum_up,
        sum_down,
    )


def solution(mesh):
    return jax.shard_map(
        per_device,
        mesh=mesh,
        in_specs=(
            P(("replica", "shard"), None),
            P(("replica", "shard")),
            P(("replica", "shard"), None),
            P("shard"),
            P("shard", None),
            P("shard", None),
            P("shard", None),
            P("shard", None),
            P("shard", None),
            P("shard", None),
            P("shard"),
            P("shard"),
            P("shard", None),
            P("shard"),
            P("shard", None),
            P("shard", None),
            P("shard", None),
        ),
        out_specs=(
            P(("replica", "shard"), None),
            P(("replica", "shard"), None),
            P("shard"),
            P("shard", None),
            P("shard", None),
            P("shard", None),
            P("shard", None),
            P("shard", None),
            P("shard", None),
            P("shard"),
            P("shard"),
            P("shard", None),
            P("shard"),
            P("shard", None),
            P("shard", None),
            P("shard", None),
        ),
        check_vma=False,
    )
```

```python
import functools

import jax
import jax.numpy as jnp
from jax import lax
from jax.experimental import pallas as pl
from jax.experimental.pallas import tpu as pltpu
from jax.sharding import PartitionSpec as P

HEAD_COUNT = 4
DK = 128
VALUE_WIDTH = 256
BLOCK = 64
KD = HEAD_COUNT * DK
VD = HEAD_COUNT * VALUE_WIDTH
EVERY = ("replica", "shard")
ROWS = ("shard", "replica")
SIDE = 128
TAIL = 8

epsilon = 1e-05
normalizer = 16.0
highest = lax.Precision.HIGHEST
high = lax.Precision.HIGH


def dense(left, right):
    return jnp.dot(left, right, preferred_element_type=jnp.float32)


def dense_back(grad_rows, weight):
    return lax.dot_general(
        grad_rows, weight, (((1,), (1,)), ((), ())), preferred_element_type=jnp.float32
    )


def dense_left(input_rows, grad_rows):
    return lax.dot_general(
        input_rows, grad_rows, (((0,), (0,)), ((), ())), preferred_element_type=jnp.float32
    )


def rms_norm(values, gain):
    return values * lax.rsqrt(jnp.mean(values * values, axis=-1, keepdims=True) + epsilon) * gain


def output_gate(mixed_rows, outgate, head_gain):
    count_of_rows = mixed_rows.shape[0]
    shaped = rms_norm(
        mixed_rows.reshape(count_of_rows, HEAD_COUNT, VALUE_WIDTH), head_gain
    ).reshape(count_of_rows, HEAD_COUNT * VALUE_WIDTH)
    return shaped * jax.nn.silu(outgate)


def swiglu(gate_pre, up_pre):
    return jax.nn.silu(gate_pre) * up_pre


def halves(a):
    if a.dtype == jnp.bfloat16:
        return (a, None)
    top = a.astype(jnp.bfloat16)
    return (top, (a - top.astype(jnp.float32)).astype(jnp.bfloat16))


def product(left, right, dims):
    def one(a, b):
        return lax.dot_general(a, b, (dims, ((), ())), preferred_element_type=jnp.float32)

    total = one(left[0], right[0])
    if left[1] is not None:
        total = total + one(left[1], right[0])
    if right[1] is not None:
        total = total + one(left[0], right[1])
    return total


def exact(left, right):
    return lax.dot_general(
        left, right, (NT, ((), ())), precision=highest, preferred_element_type=jnp.float32
    )


NN = ((1,), (0,))
NT = ((1,), (1,))
TN = ((0,), (0,))


def causal_mask():
    rows = lax.broadcasted_iota(jnp.int32, (BLOCK, BLOCK), 0)
    cols = lax.broadcasted_iota(jnp.int32, (BLOCK, BLOCK), 1)
    return rows >= cols


def forward_kernel(start_ref, qkv_ref, cumul_ref, incoming_ref, mixed_ref, saved_ref, state_ref):
    block = pl.program_id(0)

    @pl.when(block == 0)
    def _():
        state_ref[...] = incoming_ref[...].astype(jnp.float32)

    keep = jnp.where(block * BLOCK == start_ref[0], 0.0, 1.0)
    causal = causal_mask()
    for h in range(HEAD_COUNT):
        ks = slice(h * DK, (h + 1) * DK)
        vs = slice(h * VALUE_WIDTH, (h + 1) * VALUE_WIDTH)
        query = qkv_ref[:, ks].astype(jnp.float32)
        key = qkv_ref[:, KD + h * DK : KD + (h + 1) * DK].astype(jnp.float32)
        value = qkv_ref[:, 2 * KD + h * VALUE_WIDTH : 2 * KD + (h + 1) * VALUE_WIDTH]
        cumul = cumul_ref[:, ks]
        stop = cumul[BLOCK - 1 :, :]
        state = state_ref[vs, :] * keep
        saved_ref[0, vs, :] = state
        query_f = query * jnp.exp(cumul)
        key_f = key * jnp.exp(-cumul)
        query_dec = halves(query_f)
        key_end = halves(key * jnp.exp(stop - cumul))
        scores = jnp.where(causal, exact(query_f, key_f), 0.0)
        mixed_ref[:, vs] = product(query_dec, halves(state), NT) + product(
            halves(scores), (value, None), NN
        )
        state_ref[vs, :] = state * jnp.exp(stop) + product((value, None), key_end, TN)


def backward_kernel(
    start_ref, qkv_ref, cumul_ref, grad_ref, saved_ref, outgoing_ref, gqkv_ref, gdecay_ref, back_ref
):
    step = pl.program_id(0)
    block = pl.num_programs(0) - 1 - step

    @pl.when(step == 0)
    def _():
        back_ref[...] = outgoing_ref[...].astype(jnp.float32)

    keep = jnp.where(block * BLOCK == start_ref[0], 0.0, 1.0)
    causal = causal_mask()
    suffix = jnp.where(
        lax.broadcasted_iota(jnp.int32, (BLOCK, BLOCK), 0)
        <= lax.broadcasted_iota(jnp.int32, (BLOCK, BLOCK), 1),
        1.0,
        0.0,
    )
    last = lax.broadcasted_iota(jnp.int32, (BLOCK, DK), 0) == BLOCK - 1
    for h in range(HEAD_COUNT):
        ks = slice(h * DK, (h + 1) * DK)
        ks2 = slice(KD + h * DK, KD + (h + 1) * DK)
        vs = slice(h * VALUE_WIDTH, (h + 1) * VALUE_WIDTH)
        vs2 = slice(2 * KD + h * VALUE_WIDTH, 2 * KD + (h + 1) * VALUE_WIDTH)
        query = qkv_ref[:, ks].astype(jnp.float32)
        key = qkv_ref[:, ks2].astype(jnp.float32)
        value = (qkv_ref[:, vs2], None)
        cumul = cumul_ref[:, ks]
        stop = cumul[BLOCK - 1 :, :]
        grow = jnp.exp(cumul)
        shrink = jnp.exp(-cumul)
        to_end = jnp.exp(stop - cumul)
        whole = jnp.exp(stop)
        query_f = query * grow
        key_f = key * shrink
        end_f = key * to_end
        query_dec = halves(query_f)
        key_dec = halves(key_f)
        key_end = halves(end_f)
        grad_f = grad_ref[:, vs]
        grad = halves(grad_f)
        rest = (grad_f - grad[0].astype(jnp.float32)) - grad[1].astype(jnp.float32)
        grad_value = product(grad, value, NT) + product(
            (rest.astype(jnp.bfloat16), None), value, NT
        )
        state_f = saved_ref[0, vs, :]
        back_f = back_ref[vs, :]
        state = halves(state_f)
        back = halves(back_f)
        scores = halves(jnp.where(causal, product(query_dec, key_dec, NT), 0.0))
        pull = halves(jnp.where(causal, grad_value, 0.0))
        g_query_dec = product(grad, state, NN) + product(pull, key_dec, NN)
        g_key_dec = product(pull, query_dec, TN)
        g_key_end = product(value, back, NN)
        g_value = product(scores, grad, TN) + product(key_end, back, NT)
        gqkv_ref[:, ks] = (g_query_dec * grow).astype(jnp.bfloat16)
        gqkv_ref[:, ks2] = (g_key_dec * shrink + g_key_end * to_end).astype(jnp.bfloat16)
        gqkv_ref[:, vs2] = g_value.astype(jnp.bfloat16)
        end_part = g_key_end * end_f
        at_stop = jnp.sum(end_part, axis=0, keepdims=True) + whole * jnp.sum(
            state_f * back_f, axis=0, keepdims=True
        )
        g_cumul = g_query_dec * query_f - g_key_dec * key_f - end_part
        g_cumul = g_cumul + jnp.where(last, at_stop, 0.0)
        gdecay_ref[:, ks] = lax.dot_general(
            suffix, g_cumul, (NN, ((), ())), precision=highest, preferred_element_type=jnp.float32
        )
        back_ref[vs, :] = (back_f * whole + product(grad, query_dec, TN)) * keep


def rows_spec(width, index):
    return pl.BlockSpec((BLOCK, width), index)


def mix_forward(start, qkv, cumul, incoming):
    count = qkv.shape[0] // BLOCK
    place = lambda i, s: (i, 0)
    return pl.pallas_call(
        forward_kernel,
        grid_spec=pltpu.PrefetchScalarGridSpec(
            num_scalar_prefetch=1,
            grid=(count,),
            in_specs=[
                rows_spec(2 * KD + VD, place),
                rows_spec(KD, place),
                pl.BlockSpec((VD, DK), lambda i, s: (0, 0)),
            ],
            out_specs=[
                rows_spec(VD, place),
                pl.BlockSpec((1, VD, DK), lambda i, s: (i, 0, 0)),
            ],
            scratch_shapes=[pltpu.VMEM((VD, DK), jnp.float32)],
        ),
        out_shape=[
            jax.ShapeDtypeStruct((count * BLOCK, VD), jnp.float32),
            jax.ShapeDtypeStruct((count, VD, DK), jnp.float32),
        ],
        name="mix_forward",
    )(start, qkv, cumul, incoming)


def mix_backward(start, qkv, cumul, grad, saved, outgoing):
    count = qkv.shape[0] // BLOCK
    place = lambda i, s: (count - 1 - i, 0)
    return pl.pallas_call(
        backward_kernel,
        grid_spec=pltpu.PrefetchScalarGridSpec(
            num_scalar_prefetch=1,
            grid=(count,),
            in_specs=[
                rows_spec(2 * KD + VD, place),
                rows_spec(KD, place),
                rows_spec(VD, place),
                pl.BlockSpec((1, VD, DK), lambda i, s: (count - 1 - i, 0, 0)),
                pl.BlockSpec((VD, DK), lambda i, s: (0, 0)),
            ],
            out_specs=[
                rows_spec(2 * KD + VD, place),
                rows_spec(KD, place),
            ],
            scratch_shapes=[pltpu.VMEM((VD, DK), jnp.float32)],
        ),
        out_shape=[
            jax.ShapeDtypeStruct((count * BLOCK, 2 * KD + VD), jnp.bfloat16),
            jax.ShapeDtypeStruct((count * BLOCK, KD), jnp.float32),
        ],
        name="mix_backward",
    )(start, qkv, cumul, grad, saved, outgoing)


def chain(pieces, decays, reverse):
    count = pieces.shape[0]

    def kernel(pieces_ref, decays_ref, out_ref):
        def one(step, state):
            at = count - 1 - step if reverse else step
            out_ref[at] = state.astype(jnp.bfloat16)
            return decays_ref[at] * state + pieces_ref[at].astype(jnp.float32)

        lax.fori_loop(0, count, one, jnp.zeros(pieces.shape[1:], jnp.float32))

    return pl.pallas_call(
        kernel,
        out_shape=jax.ShapeDtypeStruct(pieces.shape, jnp.bfloat16),
        name="chain_back" if reverse else "chain",
    )(pieces, decays)


def device_count():
    return lax.axis_size("replica") * lax.axis_size("shard")


def exchange_with_decay(state, decay):
    count = device_count()
    rows = VD // count
    top = decay.astype(jnp.bfloat16)
    rest = decay - top.astype(jnp.float32)
    middle = rest.astype(jnp.bfloat16)
    low = (rest - middle.astype(jnp.float32)).astype(jnp.bfloat16)
    terms = jnp.stack([top, middle, low]).reshape(3, HEAD_COUNT, DK).transpose(1, 0, 2)
    terms = jnp.pad(terms, ((0, 0), (0, TAIL - 3), (0, 0)))
    terms = jnp.repeat(terms, count // HEAD_COUNT, axis=0)
    sent = jnp.concatenate([state.astype(jnp.bfloat16).reshape(count, rows, DK), terms], axis=1)
    got = lax.all_to_all(sent, EVERY, 0, 0)
    decays = jnp.sum(got[:, rows : rows + 3].astype(jnp.float32), axis=1, keepdims=True)
    folded = chain(got[:, :rows], decays, False)
    return lax.all_to_all(folded, EVERY, 0, 0).reshape(VD, DK), decays


def exchange_back(state, decays):
    count = device_count()
    pieces = lax.all_to_all(
        state.astype(jnp.bfloat16).reshape(count, VD // count, DK), EVERY, 0, 0
    )
    folded = chain(pieces, decays, True)
    return lax.all_to_all(folded, EVERY, 0, 0).reshape(VD, DK)


def fetch(shard):
    piece = shard.shape[0] // lax.axis_size("replica")
    mine = lax.dynamic_slice_in_dim(shard, lax.axis_index("replica") * piece, piece, 0)
    return lax.all_gather(mine, ROWS, axis=0, tiled=True)


MESH = pl.DeviceIdType.MESH


def gather_kernel(shards, parts, piece_ref, whole_ref, local_sem, send_sem, recv_sem):
    at_z = lax.axis_index("shard")
    at_p = lax.axis_index("replica")
    core, at_x, at_y = at_p % 2, (at_p // 2) % 2, at_p // 4
    rows, width = piece_ref.shape
    small = rows // 8
    by_core = at_p + 1 - 2 * core
    by_x = at_p + 2 - 4 * at_x
    by_y = at_p + 4 - 8 * at_y
    plans = []
    low = 0
    for turn in range(parts):
        size = width // 128 * (turn + 1) // parts * 128 - low
        if turn % 2 == 0:
            plans.append((low, size, core * 4 + at_y * 2 + at_x, (by_x, by_y, by_core)))
        else:
            plans.append((low, size, core * 4 + at_x * 2 + at_y, (by_y, by_x, by_core)))
        low += size

    barrier = pltpu.get_barrier_semaphore()
    for step in range(1, shards):
        pl.semaphore_signal(
            barrier, inc=1, device_id=(at_p, (at_z + step) % shards), device_id_type=MESH
        )
    for partner in (by_core, by_x, by_y):
        pl.semaphore_signal(barrier, inc=1, device_id=(partner, at_z), device_id_type=MESH)
    pl.semaphore_wait(barrier, shards + 2)

    def place(owner, half, block, count):
        start = pl.multiple_of(owner * rows + block * small, small)
        low, size = plans[half][:2]
        return whole_ref.at[pl.ds(start, count * small), pl.ds(low, size)]

    def copy(source, target, step, half, stage, device):
        return pltpu.make_async_remote_copy(
            src_ref=source,
            dst_ref=target,
            send_sem=send_sem.at[step - 1, half, stage],
            recv_sem=recv_sem.at[step - 1, half, stage],
            device_id=device,
            device_id_type=MESH,
        )

    def first(step, half):
        low, size, block, _ = plans[half]
        source = piece_ref.at[pl.ds(pl.multiple_of(block * small, small), small), pl.ds(low, size)]
        target = place(at_z, half, block, 1)
        return copy(source, target, step, half, 0, (at_p, (at_z + step) % shards))

    def own_block(half, stage):
        block = plans[half][2]
        return block - block % (1 << stage)

    def other_block(half, stage):
        block = own_block(half, stage)
        size = 1 << stage
        return block + size - 2 * size * ((block // size) % 2)

    def later(step, half, stage):
        owner = (at_z + shards - step) % shards
        region = place(owner, half, own_block(half, stage), 1 << stage)
        return copy(region, region, step, half, stage + 1, (plans[half][3][stage], at_z))

    def arrived(step, half, stage):
        owner = (at_z + shards - step) % shards
        if stage < 0:
            region = place(owner, half, plans[half][2], 1)
        else:
            region = place(owner, half, other_block(half, stage), 1 << stage)
        copy(region, region, step, half, stage + 1, (at_p, (at_z + 1) % shards)).wait_recv()

    order = [1, shards - 1] + list(range(2, shards - 1))
    for step in order:
        for half in range(parts):
            first(step, half).start()
    local = pltpu.make_async_copy(
        piece_ref, whole_ref.at[pl.ds(pl.multiple_of(at_z * rows, rows), rows), :], local_sem
    )
    local.start()
    units = [(step, half) for step in order for half in range(parts)]
    lag = 2 if parts == 2 else 4
    for front in range(len(units) + 2 * lag):
        for stage in range(3):
            turn = front - lag * stage
            if 0 <= turn < len(units):
                arrived(*units[turn], stage - 1)
                later(*units[turn], stage).start()
    for step in order:
        for half in range(parts):
            arrived(step, half, 2)
            first(step, half).wait_send()
            for stage in range(3):
                later(step, half, stage).wait_send()
    local.wait()


def gather_now(shard, parts):
    shards = lax.axis_size("shard")
    if lax.axis_size("replica") != 8 or shard.shape[0] % 128 != 0:
        return fetch(shard)
    rows, width = shard.shape
    return pl.pallas_call(
        functools.partial(gather_kernel, shards, parts),
        in_specs=[pl.BlockSpec(memory_space=pltpu.VMEM)],
        out_specs=pl.BlockSpec(memory_space=pl.ANY),
        out_shape=jax.ShapeDtypeStruct((shards * rows, width), jnp.bfloat16),
        scratch_shapes=[
            pltpu.SemaphoreType.DMA,
            pltpu.SemaphoreType.DMA((shards - 1, parts, 4)),
            pltpu.SemaphoreType.DMA((shards - 1, parts, 4)),
        ],
        compiler_params=pltpu.CompilerParams(collective_id=0, has_side_effects=True),
        name="gather_now",
    )(shard)


def add_low(left, right):
    return (left.astype(jnp.float32) + right.astype(jnp.float32)).astype(jnp.bfloat16)


def flip(value, bit):
    size = lax.axis_size("replica")
    return lax.ppermute(value, "replica", [(i, i ^ (1 << bit)) for i in range(size)])


def bit_of(bit):
    return (lax.axis_index("replica") >> bit) & 1


def row_bits():
    return list(range(1, lax.axis_size("replica").bit_length() - 1))


def pick(view, bits, bit, other):
    at = bit_of(bit)
    return lax.dynamic_index_in_dim(view, 1 - at if other else at, 1 + bits.index(bit))


def reduce_stages(left, right):
    half = right.shape[1] // 2
    shards = lax.axis_size("shard")
    bits = row_bits()
    at = bit_of(0)
    theirs = lax.dynamic_slice_in_dim(right, (1 - at) * half, half, 1)
    mine = lax.dynamic_slice_in_dim(right, at * half, half, 1)
    (got,) = yield (flip(dense_left(left, theirs).astype(jnp.bfloat16), 0),)
    total = add_low(dense_left(left, mine), got)
    total = total.reshape((shards,) + (2,) * len(bits) + (-1, half))
    first, second = total[: shards // 2], total[shards // 2 :]
    for bit_a, bit_b in zip(bits, bits[::-1]):
        got_a = flip(pick(first, bits, bit_a, True), bit_a)
        got_b = flip(pick(second, bits, bit_b, True), bit_b)
        first, second, got_a, got_b = yield (first, second, got_a, got_b)
        first = add_low(pick(first, bits, bit_a, False), got_a)
        second = add_low(pick(second, bits, bit_b, False), got_b)
    total = jnp.concatenate([first, second], axis=0).reshape(shards, -1, half)
    (got,) = yield (lax.all_to_all(total, "shard", 0, 0),)
    part = jnp.sum(got.astype(jnp.float32), axis=0).astype(jnp.bfloat16)
    rows = part.shape[0]
    part = part.reshape((1,) * len(bits) + (rows, half))
    first, second = part[..., : rows // 2, :], part[..., rows // 2 :, :]
    for bit_a, bit_b in zip(bits, bits[::-1]):
        first, second, got_a, got_b = yield (
            first,
            second,
            flip(first, bit_a),
            flip(second, bit_b),
        )
        first = joined_pair(first, got_a, bit_a, bits.index(bit_a))
        second = joined_pair(second, got_b, bit_b, bits.index(bit_b))
    whole = jnp.concatenate([first, second], axis=len(bits)).reshape(-1, half)
    whole, got = yield (whole, flip(whole, 0))
    low = bit_of(0) == 0
    return jnp.where(low, whole, got), jnp.where(low, got, whole)


def joined_pair(mine, got, bit, axis):
    return jnp.where(
        bit_of(bit) == 0,
        jnp.concatenate([mine, got], axis),
        jnp.concatenate([got, mine], axis),
    )


class Reduction:
    def __init__(self, left, right):
        self.stages = reduce_stages(left, right)
        self.state = next(self.stages)
        self.result = None

    def advance(self, state):
        try:
            self.state = self.stages.send(state)
        except StopIteration as stop:
            self.state, self.result = None, stop.value


def tie(values, jobs):
    jobs = [job for job in jobs if job.state is not None]
    tied = lax.optimization_barrier((values, [job.state for job in jobs]))
    for job, state in zip(jobs, tied[1]):
        job.advance(state)
    return tied[0]


def reduce_side(side):
    shards = lax.axis_size("shard")
    replicas = lax.axis_size("replica")
    width = side.shape[1]
    sent = side.astype(jnp.bfloat16).reshape(shards, replicas, -1, width).transpose(1, 0, 2, 3)
    got = lax.all_to_all(sent.reshape(shards * replicas, -1, width), EVERY, 0, 0)
    part = jnp.sum(got.astype(jnp.float32), axis=0).astype(jnp.bfloat16)
    spread = jnp.broadcast_to(part[None], (replicas,) + part.shape)
    return lax.all_to_all(spread, "replica", 0, 0).reshape(-1, width)


def column(vector, rows):
    return jnp.pad(vector, (0, rows - vector.shape[0]))[:, None]


def per_device(
    tokens,
    seq_start,
    out_grad,
    norm_gain,
    w_query,
    w_key,
    w_value,
    w_outgate,
    w_lowrank,
    w_rank_up,
    gate_bias,
    head_gain,
    w_output,
    ffn_gain,
    w_gate,
    w_up,
    w_down,
):
    shards = lax.axis_size("shard")
    rows = w_query.shape[0]
    rank = w_lowrank.shape[1]
    spread = w_rank_up.size // rows
    at_norm = rank
    at_ffn = rank + 1
    at_bias = rank + 2
    at_head = rank + 3
    at_up = rank + 4
    side = jnp.concatenate(
        [
            w_lowrank,
            norm_gain[:, None],
            ffn_gain[:, None],
            column(gate_bias, rows),
            column(head_gain, rows),
            w_rank_up.reshape(rows, spread),
            jnp.zeros((rows, SIDE - at_up - spread), jnp.bfloat16),
        ],
        axis=1,
    )
    early = gather_now(
        jnp.concatenate([w_query, w_key, w_value, w_outgate, side, w_output], axis=1), 4
    )
    split = early.shape[1] - w_output.shape[1]
    mixer_w = early[:, :split]
    output_w = early[:, split:]
    gate_shard, up_shard, down_shard = (w_gate, w_up, w_down)
    gate_up_w = fetch(jnp.concatenate([gate_shard, up_shard], axis=1))
    down_w = fetch(down_shard)

    qkv_width = 2 * KD + VD
    wide = qkv_width + VD
    side_w = mixer_w[:, wide:]
    lowrank_w = side_w[:, :rank]
    gain_one = side_w[:, at_norm].astype(jnp.float32)
    gain_two = side_w[:, at_ffn].astype(jnp.float32)
    bias_full = side_w[:, at_bias].reshape(shards, rows)[:, : gate_bias.shape[0]].reshape(-1)
    head_one = (
        side_w[:, at_head].reshape(shards, rows)[:, : head_gain.shape[0]].reshape(-1)
    ).astype(jnp.float32)
    rank_up_w = side_w[:, at_up : at_up + spread].reshape(rank, KD)

    residual_in = tokens.astype(jnp.float32)
    count_of_rows = residual_in.shape[0]
    block_count = count_of_rows // BLOCK
    slice_start = seq_start[0]
    normed = rms_norm(residual_in, gain_one).astype(jnp.bfloat16)
    qkv = dense(normed, mixer_w[:, :qkv_width]).astype(jnp.bfloat16)
    outgate = dense(normed, mixer_w[:, qkv_width:wide])
    rank_rows = dense(normed, lowrank_w).astype(jnp.bfloat16)
    gate_logit = dense(rank_rows, rank_up_w) + bias_full.astype(jnp.float32)
    log_decay = jax.nn.log_sigmoid(gate_logit) / normalizer

    lower = jnp.tril(jnp.ones((BLOCK, BLOCK), jnp.float32))
    cumul3 = jnp.einsum(
        "ij,bjk->bik", lower, log_decay.reshape(block_count, BLOCK, KD), precision=highest
    )
    stops = cumul3[:, -1]
    strict = jnp.tril(jnp.ones((block_count, block_count), jnp.float32), -1)
    ahead_of = jnp.dot(strict, stops, precision=highest)
    after = jnp.dot(strict.T, stops, precision=highest)
    cumul = cumul3.reshape(count_of_rows, KD)
    query_f = qkv[:, :KD].astype(jnp.float32)
    key_f = qkv[:, KD : 2 * KD].astype(jnp.float32)
    value_rows = qkv[:, 2 * KD :]
    has_start = slice_start < count_of_rows
    at = jnp.arange(count_of_rows, dtype=jnp.int32)[:, None]
    to_end = jnp.exp((stops + after)[:, None, :] - cumul3).reshape(count_of_rows, KD)
    counts = jnp.logical_or(jnp.logical_not(has_start), at >= slice_start)
    key_to_end = jnp.where(counts, key_f * to_end, 0.0)
    from_first = jnp.exp(ahead_of[:, None, :] + cumul3).reshape(count_of_rows, KD)
    query_first = jnp.where(at < slice_start, query_f * from_first, 0.0)
    carry_decay = jnp.where(has_start, 0.0, jnp.exp(jnp.sum(stops, axis=0)))

    def heads(rows_of, width):
        return rows_of.reshape(count_of_rows, HEAD_COUNT, width)

    local_end = jnp.einsum(
        "thv,thk->hvk",
        heads(value_rows.astype(jnp.float32), VALUE_WIDTH),
        heads(key_to_end, DK),
        precision=high,
    ).reshape(VD, DK)
    incoming, decays = exchange_with_decay(local_end, carry_decay)
    mixed_rows, saved = mix_forward(seq_start, qkv, cumul, incoming)
    gated_rows = output_gate(mixed_rows, outgate, head_one).astype(jnp.bfloat16)
    middle = residual_in + dense(gated_rows, output_w)
    normed_ffn = rms_norm(middle, gain_two).astype(jnp.bfloat16)
    width = w_gate.shape[1]
    gate_w = gate_up_w[:, :width]
    up_w = gate_up_w[:, width:]
    gate_pre = dense(normed_ffn, gate_w)
    up_pre = dense(normed_ffn, up_w)
    hidden = swiglu(gate_pre, up_pre).astype(jnp.bfloat16)
    output = (middle + dense(hidden, down_w)).astype(jnp.bfloat16)

    grad_out = out_grad.astype(jnp.float32)
    down_sum = Reduction(hidden, out_grad)
    grad_hidden = dense_back(out_grad, down_w)
    unused, pull_swiglu = jax.vjp(swiglu, gate_pre, up_pre)
    grad_gate_f, grad_up_f = pull_swiglu(grad_hidden)
    grad_both = jnp.concatenate(
        [grad_gate_f.astype(jnp.bfloat16), grad_up_f.astype(jnp.bfloat16)], axis=1
    )
    grad_both = tie(grad_both, [down_sum])
    both_sum = Reduction(normed_ffn, grad_both)
    grad_normed_ffn = dense_back(grad_both, gate_up_w)
    unused, pull_norm_two = jax.vjp(rms_norm, middle, gain_two)
    grad_middle_part, grad_gain_two = pull_norm_two(grad_normed_ffn)
    grad_middle = grad_out + grad_middle_part
    grad_attn = grad_middle.astype(jnp.bfloat16)
    grad_attn, grad_middle = tie((grad_attn, grad_middle), [down_sum, both_sum])
    output_sum = Reduction(gated_rows, grad_attn)
    grad_gated = dense_back(grad_attn, output_w)
    unused, pull_gate = jax.vjp(output_gate, mixed_rows, outgate, head_one)
    mixed_gradient, grad_outgate_f, grad_head = pull_gate(grad_gated)
    grad_outgate = grad_outgate_f.astype(jnp.bfloat16)
    mixed_gradient, grad_outgate = tie(
        (mixed_gradient, grad_outgate), [down_sum, both_sum, output_sum]
    )
    outgate_sum = Reduction(normed, grad_outgate)
    carry_grad = jnp.einsum(
        "thv,thk->hvk",
        heads(mixed_gradient, VALUE_WIDTH),
        heads(query_first, DK),
        precision=high,
    ).reshape(VD, DK)
    outgoing = exchange_back(carry_grad, decays)
    outgoing = tie(outgoing, [down_sum, both_sum, output_sum, outgate_sum])
    grad_qkv, grad_decay = mix_backward(
        seq_start, qkv, cumul, mixed_gradient, saved, outgoing
    )
    grad_qkv, grad_decay = tie(
        (grad_qkv, grad_decay), [down_sum, both_sum, output_sum, outgate_sum]
    )
    qkv_sum = Reduction(normed, grad_qkv)
    grad_logit = (grad_decay * jax.nn.sigmoid(-gate_logit) / normalizer).astype(jnp.bfloat16)
    grad_bias = jnp.sum(grad_logit.astype(jnp.float32), axis=0)
    grad_rank_up = dense_left(rank_rows, grad_logit)
    grad_rank = dense_back(grad_logit, rank_up_w).astype(jnp.bfloat16)
    grad_mixer = jnp.concatenate(
        [grad_qkv, grad_outgate, jnp.pad(grad_rank, ((0, 0), (0, SIDE - rank)))], axis=1
    )
    grad_normed = dense_back(grad_mixer, mixer_w)

    def spread_rows(vector):
        per = vector.reshape(shards, -1)
        return jnp.pad(per, ((0, 0), (0, rows - per.shape[1]))).reshape(-1, 1)

    sums = [qkv_sum, down_sum, both_sum, output_sum, outgate_sum]
    grad_normed = tie(grad_normed, sums)
    unused, pull_norm_one = jax.vjp(rms_norm, residual_in, gain_one)
    grad_input_part, grad_gain_one = pull_norm_one(grad_normed)
    grad_tokens = (grad_middle + grad_input_part).astype(jnp.bfloat16)
    side_term = jnp.concatenate(
        [
            dense_left(normed, grad_rank),
            grad_gain_one[:, None],
            grad_gain_two[:, None],
            spread_rows(grad_bias),
            spread_rows(grad_head),
            grad_rank_up.reshape(shards * rows, spread),
            jnp.zeros((shards * rows, SIDE - at_up - spread), jnp.float32),
        ],
        axis=1,
    )
    side_sum = reduce_side(side_term).astype(jnp.float32)
    while any(job.state is not None for job in sums):
        tie((), sums)

    def final(job):
        return tuple(half.astype(jnp.float32) for half in job.result)

    def joined(job):
        return jnp.concatenate(final(job), axis=1)

    sum_down = joined(down_sum)
    sum_gate, sum_up = final(both_sum)
    sum_output = joined(output_sum)
    sum_outgate = joined(outgate_sum)
    query_key, sum_value = final(qkv_sum)
    return (
        output,
        grad_tokens,
        side_sum[:, at_norm],
        query_key[:, :KD],
        query_key[:, KD:],
        sum_value,
        sum_outgate,
        side_sum[:, :rank],
        side_sum[:, at_up : at_up + spread].reshape(w_rank_up.shape),
        side_sum[: gate_bias.shape[0], at_bias],
        side_sum[: head_gain.shape[0], at_head],
        sum_output,
        side_sum[:, at_ffn],
        sum_gate,
        sum_up,
        sum_down,
    )


def solution(mesh):
    return jax.shard_map(
        per_device,
        mesh=mesh,
        in_specs=(
            P(("replica", "shard"), None),
            P(("replica", "shard")),
            P(("replica", "shard"), None),
            P("shard"),
            P("shard", None),
            P("shard", None),
            P("shard", None),
            P("shard", None),
            P("shard", None),
            P("shard", None),
            P("shard"),
            P("shard"),
            P("shard", None),
            P("shard"),
            P("shard", None),
            P("shard", None),
            P("shard", None),
        ),
        out_specs=(
            P(("replica", "shard"), None),
            P(("replica", "shard"), None),
            P("shard"),
            P("shard", None),
            P("shard", None),
            P("shard", None),
            P("shard", None),
            P("shard", None),
            P("shard", None),
            P("shard"),
            P("shard"),
            P("shard", None),
            P("shard"),
            P("shard", None),
            P("shard", None),
            P("shard", None),
        ),
        check_vma=False,
    )
```

```python
import functools

import jax
import jax.numpy as jnp
from jax import lax
from jax.experimental import pallas as pl
from jax.experimental.layout import Layout, with_layout_constraint
from jax.experimental.pallas import tpu as pltpu
from jax.sharding import PartitionSpec as P

HEAD_COUNT = 4
DK = 128
VALUE_WIDTH = 256
BLOCK = 64
KD = HEAD_COUNT * DK
VD = HEAD_COUNT * VALUE_WIDTH
EVERY = ("replica", "shard")
ROWS = ("shard", "replica")
SIDE = 128
TAIL = 8

epsilon = 1e-05
normalizer = 16.0
highest = lax.Precision.HIGHEST
high = lax.Precision.HIGH


def dense(left, right):
    return jnp.dot(left, right, preferred_element_type=jnp.float32)


def dense_back(grad_rows, weight):
    return lax.dot_general(
        grad_rows, weight, (((1,), (1,)), ((), ())), preferred_element_type=jnp.float32
    )


def dense_left(input_rows, grad_rows):
    return lax.dot_general(
        input_rows, grad_rows, (((0,), (0,)), ((), ())), preferred_element_type=jnp.float32
    )


def row_major(value):
    return with_layout_constraint(value, Layout((0, 1)))


def rms_norm(values, gain):
    return values * lax.rsqrt(jnp.mean(values * values, axis=-1, keepdims=True) + epsilon) * gain


def swiglu(gate_pre, up_pre):
    return jax.nn.silu(gate_pre) * up_pre


def halves(a):
    if a.dtype == jnp.bfloat16:
        return (a, None)
    top = a.astype(jnp.bfloat16)
    return (top, (a - top.astype(jnp.float32)).astype(jnp.bfloat16))


def product(left, right, dims):
    def one(a, b):
        return lax.dot_general(a, b, (dims, ((), ())), preferred_element_type=jnp.float32)

    total = one(left[0], right[0])
    if left[1] is not None:
        total = total + one(left[1], right[0])
    if right[1] is not None:
        total = total + one(left[0], right[1])
    return total


def exact(left, right):
    return lax.dot_general(
        left, right, (NT, ((), ())), precision=highest, preferred_element_type=jnp.float32
    )


NN = ((1,), (0,))
NT = ((1,), (1,))
TN = ((0,), (0,))


def causal_mask():
    rows = lax.broadcasted_iota(jnp.int32, (BLOCK, BLOCK), 0)
    cols = lax.broadcasted_iota(jnp.int32, (BLOCK, BLOCK), 1)
    return rows >= cols


def forward_kernel(
    start_ref,
    qkv_ref,
    cumul_ref,
    incoming_ref,
    outgate_ref,
    gain_ref,
    mixed_ref,
    saved_ref,
    gated_ref,
    state_ref,
):
    block = pl.program_id(0)

    @pl.when(block == 0)
    def _():
        state_ref[...] = incoming_ref[...].astype(jnp.float32)

    keep = jnp.where(block * BLOCK == start_ref[0], 0.0, 1.0)
    causal = causal_mask()
    for h in range(HEAD_COUNT):
        ks = slice(h * DK, (h + 1) * DK)
        vs = slice(h * VALUE_WIDTH, (h + 1) * VALUE_WIDTH)
        query = qkv_ref[:, ks].astype(jnp.float32)
        key = qkv_ref[:, KD + h * DK : KD + (h + 1) * DK].astype(jnp.float32)
        value = qkv_ref[:, 2 * KD + h * VALUE_WIDTH : 2 * KD + (h + 1) * VALUE_WIDTH]
        cumul = cumul_ref[:, ks]
        stop = cumul[BLOCK - 1 :, :]
        state = state_ref[vs, :] * keep
        saved_ref[0, vs, :] = state
        query_f = query * jnp.exp(cumul)
        key_f = key * jnp.exp(-cumul)
        query_dec = halves(query_f)
        key_end = halves(key * jnp.exp(stop - cumul))
        scores = jnp.where(causal, exact(query_f, key_f), 0.0)
        mixed = product(query_dec, halves(state), NT) + product(
            halves(scores), (value, None), NN
        )
        mixed_ref[:, vs] = mixed
        outgate = outgate_ref[:, vs]
        shaped = rms_norm(mixed, gain_ref[...])
        gated_ref[:, vs] = (shaped * (outgate * jax.nn.sigmoid(outgate))).astype(jnp.bfloat16)
        state_ref[vs, :] = state * jnp.exp(stop) + product((value, None), key_end, TN)


def backward_kernel(
    start_ref, qkv_ref, cumul_ref, grad_ref, saved_ref, outgoing_ref, gqkv_ref, gdecay_ref, back_ref
):
    step = pl.program_id(0)
    block = pl.num_programs(0) - 1 - step

    @pl.when(step == 0)
    def _():
        back_ref[...] = outgoing_ref[...].astype(jnp.float32)

    keep = jnp.where(block * BLOCK == start_ref[0], 0.0, 1.0)
    causal = causal_mask()
    suffix = jnp.where(
        lax.broadcasted_iota(jnp.int32, (BLOCK, BLOCK), 0)
        <= lax.broadcasted_iota(jnp.int32, (BLOCK, BLOCK), 1),
        1.0,
        0.0,
    )
    last = lax.broadcasted_iota(jnp.int32, (BLOCK, DK), 0) == BLOCK - 1
    for h in range(HEAD_COUNT):
        ks = slice(h * DK, (h + 1) * DK)
        ks2 = slice(KD + h * DK, KD + (h + 1) * DK)
        vs = slice(h * VALUE_WIDTH, (h + 1) * VALUE_WIDTH)
        vs2 = slice(2 * KD + h * VALUE_WIDTH, 2 * KD + (h + 1) * VALUE_WIDTH)
        query = qkv_ref[:, ks].astype(jnp.float32)
        key = qkv_ref[:, ks2].astype(jnp.float32)
        value = (qkv_ref[:, vs2], None)
        cumul = cumul_ref[:, ks]
        stop = cumul[BLOCK - 1 :, :]
        grow = jnp.exp(cumul)
        shrink = jnp.exp(-cumul)
        to_end = jnp.exp(stop - cumul)
        whole = jnp.exp(stop)
        query_f = query * grow
        key_f = key * shrink
        end_f = key * to_end
        query_dec = halves(query_f)
        key_dec = halves(key_f)
        key_end = halves(end_f)
        grad_f = grad_ref[:, vs]
        grad = halves(grad_f)
        rest = (grad_f - grad[0].astype(jnp.float32)) - grad[1].astype(jnp.float32)
        grad_value = product(grad, value, NT) + product(
            (rest.astype(jnp.bfloat16), None), value, NT
        )
        state_f = saved_ref[0, vs, :]
        back_f = back_ref[vs, :]
        state = halves(state_f)
        back = halves(back_f)
        scores = halves(jnp.where(causal, product(query_dec, key_dec, NT), 0.0))
        pull = halves(jnp.where(causal, grad_value, 0.0))
        g_query_dec = product(grad, state, NN) + product(pull, key_dec, NN)
        g_key_dec = product(pull, query_dec, TN)
        g_key_end = product(value, back, NN)
        g_value = product(scores, grad, TN) + product(key_end, back, NT)
        gqkv_ref[:, ks] = (g_query_dec * grow).astype(jnp.bfloat16)
        gqkv_ref[:, ks2] = (g_key_dec * shrink + g_key_end * to_end).astype(jnp.bfloat16)
        gqkv_ref[:, vs2] = g_value.astype(jnp.bfloat16)
        end_part = g_key_end * end_f
        at_stop = jnp.sum(end_part, axis=0, keepdims=True) + whole * jnp.sum(
            state_f * back_f, axis=0, keepdims=True
        )
        g_cumul = g_query_dec * query_f - g_key_dec * key_f - end_part
        g_cumul = g_cumul + jnp.where(last, at_stop, 0.0)
        gdecay_ref[:, ks] = lax.dot_general(
            suffix, g_cumul, (NN, ((), ())), precision=highest, preferred_element_type=jnp.float32
        )
        back_ref[vs, :] = (back_f * whole + product(grad, query_dec, TN)) * keep


def rows_spec(width, index):
    return pl.BlockSpec((BLOCK, width), index)


def mix_forward(start, qkv, cumul, incoming, outgate, head_gain):
    count = qkv.shape[0] // BLOCK
    place = lambda i, s: (i, 0)
    return pl.pallas_call(
        forward_kernel,
        grid_spec=pltpu.PrefetchScalarGridSpec(
            num_scalar_prefetch=1,
            grid=(count,),
            in_specs=[
                rows_spec(2 * KD + VD, place),
                rows_spec(KD, place),
                pl.BlockSpec((VD, DK), lambda i, s: (0, 0)),
                rows_spec(VD, place),
                pl.BlockSpec((1, VALUE_WIDTH), lambda i, s: (0, 0)),
            ],
            out_specs=[
                rows_spec(VD, place),
                pl.BlockSpec((1, VD, DK), lambda i, s: (i, 0, 0)),
                rows_spec(VD, place),
            ],
            scratch_shapes=[pltpu.VMEM((VD, DK), jnp.float32)],
        ),
        out_shape=[
            jax.ShapeDtypeStruct((count * BLOCK, VD), jnp.float32),
            jax.ShapeDtypeStruct((count, VD, DK), jnp.float32),
            jax.ShapeDtypeStruct((count * BLOCK, VD), jnp.bfloat16),
        ],
        name="mix_forward",
    )(start, qkv, cumul, incoming, outgate, head_gain[None, :])


def gate_kernel(
    mixed_ref, outgate_ref, grad_ref, query_ref, gain_ref, gmixed_ref, gout_ref, carry_ref, ghead_ref
):
    @pl.when(pl.program_id(0) == 0)
    def _():
        carry_ref[...] = jnp.zeros_like(carry_ref)
        ghead_ref[...] = jnp.zeros_like(ghead_ref)

    gain = gain_ref[...]
    for h in range(HEAD_COUNT):
        ks = slice(h * DK, (h + 1) * DK)
        vs = slice(h * VALUE_WIDTH, (h + 1) * VALUE_WIDTH)
        mixed = mixed_ref[:, vs]
        outgate = outgate_ref[:, vs]
        grad = grad_ref[:, vs]
        scale = lax.rsqrt(jnp.mean(mixed * mixed, axis=-1, keepdims=True) + epsilon)
        unit = mixed * scale
        sigmoid = jax.nn.sigmoid(outgate)
        grad_shaped = grad * (outgate * sigmoid)
        gout_ref[:, vs] = (
            grad * (unit * gain) * (sigmoid * (1.0 + outgate * (1.0 - sigmoid)))
        ).astype(jnp.bfloat16)
        ghead_ref[...] += jnp.sum(grad_shaped * unit, axis=0, keepdims=True)
        grad_unit = grad_shaped * gain
        gmixed = scale * (
            grad_unit - unit * jnp.mean(grad_unit * unit, axis=-1, keepdims=True)
        )
        gmixed_ref[:, vs] = gmixed
        carry_ref[vs, :] += product(halves(gmixed), halves(query_ref[:, ks]), TN)


def gate_backward(mixed, outgate, grad, query, head_gain):
    rows = mixed.shape[0]
    block = 2 * BLOCK
    place = lambda i: (i, 0)
    fixed = lambda i: (0, 0)
    wide = pl.BlockSpec((block, VD), place)
    return pl.pallas_call(
        gate_kernel,
        grid=(rows // block,),
        in_specs=[
            wide,
            wide,
            wide,
            pl.BlockSpec((block, KD), place),
            pl.BlockSpec((1, VALUE_WIDTH), fixed),
        ],
        out_specs=[
            wide,
            wide,
            pl.BlockSpec((VD, DK), fixed),
            pl.BlockSpec((1, VALUE_WIDTH), fixed),
        ],
        out_shape=[
            jax.ShapeDtypeStruct((rows, VD), jnp.float32),
            jax.ShapeDtypeStruct((rows, VD), jnp.bfloat16),
            jax.ShapeDtypeStruct((VD, DK), jnp.float32),
            jax.ShapeDtypeStruct((1, VALUE_WIDTH), jnp.float32),
        ],
        name="gate_backward",
    )(mixed, outgate, grad, query, head_gain[None, :])


def mix_backward(start, qkv, cumul, grad, saved, outgoing):
    count = qkv.shape[0] // BLOCK
    place = lambda i, s: (count - 1 - i, 0)
    return pl.pallas_call(
        backward_kernel,
        grid_spec=pltpu.PrefetchScalarGridSpec(
            num_scalar_prefetch=1,
            grid=(count,),
            in_specs=[
                rows_spec(2 * KD + VD, place),
                rows_spec(KD, place),
                rows_spec(VD, place),
                pl.BlockSpec((1, VD, DK), lambda i, s: (count - 1 - i, 0, 0)),
                pl.BlockSpec((VD, DK), lambda i, s: (0, 0)),
            ],
            out_specs=[
                rows_spec(2 * KD + VD, place),
                rows_spec(KD, place),
            ],
            scratch_shapes=[pltpu.VMEM((VD, DK), jnp.float32)],
        ),
        out_shape=[
            jax.ShapeDtypeStruct((count * BLOCK, 2 * KD + VD), jnp.bfloat16),
            jax.ShapeDtypeStruct((count * BLOCK, KD), jnp.float32),
        ],
        name="mix_backward",
    )(start, qkv, cumul, grad, saved, outgoing)


def chain(pieces, decays, reverse):
    count = pieces.shape[0]

    def kernel(pieces_ref, decays_ref, out_ref):
        def one(step, state):
            at = count - 1 - step if reverse else step
            out_ref[at] = state.astype(jnp.bfloat16)
            return decays_ref[at] * state + pieces_ref[at].astype(jnp.float32)

        lax.fori_loop(0, count, one, jnp.zeros(pieces.shape[1:], jnp.float32))

    return pl.pallas_call(
        kernel,
        out_shape=jax.ShapeDtypeStruct(pieces.shape, jnp.bfloat16),
        name="chain_back" if reverse else "chain",
    )(pieces, decays)


def device_count():
    return lax.axis_size("replica") * lax.axis_size("shard")


def exchange_with_decay(state, decay):
    count = device_count()
    rows = VD // count
    top = decay.astype(jnp.bfloat16)
    rest = decay - top.astype(jnp.float32)
    middle = rest.astype(jnp.bfloat16)
    low = (rest - middle.astype(jnp.float32)).astype(jnp.bfloat16)
    terms = jnp.stack([top, middle, low]).reshape(3, HEAD_COUNT, DK).transpose(1, 0, 2)
    terms = jnp.pad(terms, ((0, 0), (0, TAIL - 3), (0, 0)))
    terms = jnp.repeat(terms, count // HEAD_COUNT, axis=0)
    sent = jnp.concatenate([state.astype(jnp.bfloat16).reshape(count, rows, DK), terms], axis=1)
    got = lax.all_to_all(sent, EVERY, 0, 0)
    decays = jnp.sum(got[:, rows : rows + 3].astype(jnp.float32), axis=1, keepdims=True)
    folded = chain(got[:, :rows], decays, False)
    return lax.all_to_all(folded, EVERY, 0, 0).reshape(VD, DK), decays


def exchange_back(state, decays):
    count = device_count()
    pieces = lax.all_to_all(
        state.astype(jnp.bfloat16).reshape(count, VD // count, DK), EVERY, 0, 0
    )
    folded = chain(pieces, decays, True)
    return lax.all_to_all(folded, EVERY, 0, 0).reshape(VD, DK)


def fetch(shard):
    piece = shard.shape[0] // lax.axis_size("replica")
    mine = lax.dynamic_slice_in_dim(shard, lax.axis_index("replica") * piece, piece, 0)
    return lax.all_gather(mine, ROWS, axis=0, tiled=True)


MESH = pl.DeviceIdType.MESH


def gather_kernel(shards, parts, piece_ref, whole_ref, local_sem, send_sem, recv_sem):
    at_z = lax.axis_index("shard")
    at_p = lax.axis_index("replica")
    core, at_x, at_y = at_p % 2, (at_p // 2) % 2, at_p // 4
    rows, width = piece_ref.shape
    small = rows // 8
    by_core = at_p + 1 - 2 * core
    by_x = at_p + 2 - 4 * at_x
    by_y = at_p + 4 - 8 * at_y
    plans = []
    low = 0
    for turn in range(parts):
        size = width // 128 * (turn + 1) // parts * 128 - low
        if turn % 2 == 0:
            plans.append((low, size, core * 4 + at_y * 2 + at_x, (by_x, by_y, by_core)))
        else:
            plans.append((low, size, core * 4 + at_x * 2 + at_y, (by_y, by_x, by_core)))
        low += size

    barrier = pltpu.get_barrier_semaphore()
    for step in range(1, shards):
        pl.semaphore_signal(
            barrier, inc=1, device_id=(at_p, (at_z + step) % shards), device_id_type=MESH
        )
    for partner in (by_core, by_x, by_y):
        pl.semaphore_signal(barrier, inc=1, device_id=(partner, at_z), device_id_type=MESH)
    pl.semaphore_wait(barrier, shards + 2)

    def place(owner, half, block, count):
        start = pl.multiple_of(owner * rows + block * small, small)
        low, size = plans[half][:2]
        return whole_ref.at[pl.ds(start, count * small), pl.ds(low, size)]

    def copy(source, target, step, half, stage, device):
        return pltpu.make_async_remote_copy(
            src_ref=source,
            dst_ref=target,
            send_sem=send_sem.at[step - 1, half, stage],
            recv_sem=recv_sem.at[step - 1, half, stage],
            device_id=device,
            device_id_type=MESH,
        )

    def first(step, half):
        low, size, block, _ = plans[half]
        source = piece_ref.at[pl.ds(pl.multiple_of(block * small, small), small), pl.ds(low, size)]
        target = place(at_z, half, block, 1)
        return copy(source, target, step, half, 0, (at_p, (at_z + step) % shards))

    def own_block(half, stage):
        block = plans[half][2]
        return block - block % (1 << stage)

    def other_block(half, stage):
        block = own_block(half, stage)
        size = 1 << stage
        return block + size - 2 * size * ((block // size) % 2)

    def later(step, half, stage):
        owner = (at_z + shards - step) % shards
        region = place(owner, half, own_block(half, stage), 1 << stage)
        return copy(region, region, step, half, stage + 1, (plans[half][3][stage], at_z))

    def arrived(step, half, stage):
        owner = (at_z + shards - step) % shards
        if stage < 0:
            region = place(owner, half, plans[half][2], 1)
        else:
            region = place(owner, half, other_block(half, stage), 1 << stage)
        copy(region, region, step, half, stage + 1, (at_p, (at_z + 1) % shards)).wait_recv()

    order = [1, shards - 1] + list(range(2, shards - 1))
    for step in order:
        for half in range(parts):
            first(step, half).start()
    local = pltpu.make_async_copy(
        piece_ref, whole_ref.at[pl.ds(pl.multiple_of(at_z * rows, rows), rows), :], local_sem
    )
    local.start()
    units = [(step, half) for step in order for half in range(parts)]
    lag = 2 if parts == 2 else 4
    for front in range(len(units) + 2 * lag):
        for stage in range(3):
            turn = front - lag * stage
            if 0 <= turn < len(units):
                arrived(*units[turn], stage - 1)
                later(*units[turn], stage).start()
    for step in order:
        for half in range(parts):
            arrived(step, half, 2)
            first(step, half).wait_send()
            for stage in range(3):
                later(step, half, stage).wait_send()
    local.wait()


def gather_now(shard, parts):
    shards = lax.axis_size("shard")
    if lax.axis_size("replica") != 8 or shard.shape[0] % 128 != 0:
        return fetch(shard)
    rows, width = shard.shape
    return pl.pallas_call(
        functools.partial(gather_kernel, shards, parts),
        in_specs=[pl.BlockSpec(memory_space=pltpu.VMEM)],
        out_specs=pl.BlockSpec(memory_space=pl.ANY),
        out_shape=jax.ShapeDtypeStruct((shards * rows, width), jnp.bfloat16),
        scratch_shapes=[
            pltpu.SemaphoreType.DMA,
            pltpu.SemaphoreType.DMA((shards - 1, parts, 4)),
            pltpu.SemaphoreType.DMA((shards - 1, parts, 4)),
        ],
        compiler_params=pltpu.CompilerParams(collective_id=0, has_side_effects=True),
        name="gather_now",
    )(shard)


def add_low(left, right):
    return (left.astype(jnp.float32) + right.astype(jnp.float32)).astype(jnp.bfloat16)


def flip(value, bit):
    size = lax.axis_size("replica")
    return lax.ppermute(value, "replica", [(i, i ^ (1 << bit)) for i in range(size)])


def bit_of(bit):
    return (lax.axis_index("replica") >> bit) & 1


def row_bits():
    return list(range(1, lax.axis_size("replica").bit_length() - 1))


def pick(view, bits, bit, other):
    at = bit_of(bit)
    return lax.dynamic_index_in_dim(view, 1 - at if other else at, 1 + bits.index(bit))


def column_half(right, other):
    half = right.shape[1] // 2
    at = bit_of(0)
    return lax.dynamic_slice_in_dim(right, (1 - at if other else at) * half, half, 1)


def reduce_stages(pairs):
    shards = lax.axis_size("shard")
    bits = row_bits()
    got = yield tuple(
        flip(dense_left(left, column_half(right, True)).astype(jnp.bfloat16), 0)
        for left, right in pairs
    )
    total = jnp.concatenate(
        [
            add_low(dense_left(left, column_half(right, False)), came)
            for (left, right), came in zip(pairs, got)
        ],
        axis=1,
    )
    half = total.shape[1]
    total = total.reshape((shards,) + (2,) * len(bits) + (-1, half))
    first, second = total[: shards // 2], total[shards // 2 :]
    for bit_a, bit_b in zip(bits, bits[::-1]):
        got_a = flip(pick(first, bits, bit_a, True), bit_a)
        got_b = flip(pick(second, bits, bit_b, True), bit_b)
        first, second, got_a, got_b = yield (first, second, got_a, got_b)
        first = add_low(pick(first, bits, bit_a, False), got_a)
        second = add_low(pick(second, bits, bit_b, False), got_b)
    total = jnp.concatenate([first, second], axis=0).reshape(shards, -1, half)
    (got,) = yield (lax.all_to_all(total, "shard", 0, 0),)
    part = jnp.sum(got.astype(jnp.float32), axis=0).astype(jnp.bfloat16)
    rows = part.shape[0]
    part = part.reshape((1,) * len(bits) + (rows, half))
    first, second = part[..., : rows // 2, :], part[..., rows // 2 :, :]
    for bit_a, bit_b in zip(bits, bits[::-1]):
        first, second, got_a, got_b = yield (
            first,
            second,
            flip(first, bit_a),
            flip(second, bit_b),
        )
        first = joined_pair(first, got_a, bit_a, bits.index(bit_a))
        second = joined_pair(second, got_b, bit_b, bits.index(bit_b))
    whole = jnp.concatenate([first, second], axis=len(bits)).reshape(-1, half)
    whole, got = yield (whole, flip(whole, 0))
    low = bit_of(0) == 0
    return jnp.where(low, whole, got), jnp.where(low, got, whole)


def joined_pair(mine, got, bit, axis):
    return jnp.where(
        bit_of(bit) == 0,
        jnp.concatenate([mine, got], axis),
        jnp.concatenate([got, mine], axis),
    )


class Reduction:
    def __init__(self, *pairs):
        self.stages = reduce_stages(pairs)
        self.widths = [right.shape[1] // 2 for _, right in pairs]
        self.state = next(self.stages)
        self.result = None

    def advance(self, state):
        try:
            self.state = self.stages.send(state)
        except StopIteration as stop:
            self.state, self.result = None, stop.value

    def finish(self):
        while self.state is not None:
            self.advance(self.state)
        low, high = (half.astype(jnp.float32) for half in self.result)
        parts = []
        at = 0
        for width in self.widths:
            parts.append((low[:, at : at + width], high[:, at : at + width]))
            at += width
        return parts


def tie(values, jobs):
    jobs = [job for job in jobs if job.state is not None]
    tied = lax.optimization_barrier((values, [job.state for job in jobs]))
    for job, state in zip(jobs, tied[1]):
        job.advance(state)
    return tied[0]


def reduce_side(terms):
    count = device_count()
    flat = [term.astype(jnp.bfloat16).reshape(-1, SIDE) for term in terms]
    used = sum(part.shape[0] for part in flat)
    per = -(-used // count)
    rows = jnp.pad(jnp.concatenate(flat, axis=0), ((0, count * per - used), (0, 0)))
    got = lax.all_to_all(rows.reshape(count, per, SIDE), EVERY, 0, 0)
    part = jnp.sum(got.astype(jnp.float32), axis=0).astype(jnp.bfloat16)
    spread = jnp.broadcast_to(part[None], (count, per, SIDE))
    total = lax.all_to_all(spread, EVERY, 0, 0).reshape(count * per, SIDE).astype(jnp.float32)
    sums = []
    at = 0
    for term, part in zip(terms, flat):
        sums.append(total[at : at + part.shape[0]].reshape(term.shape))
        at += part.shape[0]
    return sums


def column(vector, rows):
    return jnp.pad(vector, (0, rows - vector.shape[0]))[:, None]


def per_device(
    tokens,
    seq_start,
    out_grad,
    norm_gain,
    w_query,
    w_key,
    w_value,
    w_outgate,
    w_lowrank,
    w_rank_up,
    gate_bias,
    head_gain,
    w_output,
    ffn_gain,
    w_gate,
    w_up,
    w_down,
):
    shards = lax.axis_size("shard")
    rows = w_query.shape[0]
    rank = w_lowrank.shape[1]
    spread = w_rank_up.size // rows
    at_norm = rank
    at_ffn = rank + 1
    at_bias = rank + 2
    at_head = rank + 3
    at_up = rank + 4
    side = jnp.concatenate(
        [
            w_lowrank,
            norm_gain[:, None],
            ffn_gain[:, None],
            column(gate_bias, rows),
            column(head_gain, rows),
            w_rank_up.reshape(rows, spread),
            jnp.zeros((rows, SIDE - at_up - spread), jnp.bfloat16),
        ],
        axis=1,
    )
    early = gather_now(
        jnp.concatenate([w_query, w_key, w_value, w_outgate, side, w_output], axis=1), 4
    )
    split = early.shape[1] - w_output.shape[1]
    mixer_w = early[:, :split]
    output_w = early[:, split:]
    gate_shard, up_shard, down_shard = (w_gate, w_up, w_down)
    gate_up_w = fetch(jnp.concatenate([gate_shard, up_shard], axis=1))
    down_w = fetch(down_shard)

    qkv_width = 2 * KD + VD
    wide = qkv_width + VD
    side_w = mixer_w[:, wide:]
    lowrank_w = side_w[:, :rank]
    gain_one = side_w[:, at_norm].astype(jnp.float32)
    gain_two = side_w[:, at_ffn].astype(jnp.float32)
    bias_full = side_w[:, at_bias].reshape(shards, rows)[:, : gate_bias.shape[0]].reshape(-1)
    head_one = (
        side_w[:, at_head].reshape(shards, rows)[:, : head_gain.shape[0]].reshape(-1)
    ).astype(jnp.float32)
    rank_up_w = side_w[:, at_up : at_up + spread].reshape(rank, KD)

    residual_in = tokens.astype(jnp.float32)
    count_of_rows = residual_in.shape[0]
    block_count = count_of_rows // BLOCK
    slice_start = seq_start[0]
    normed = rms_norm(residual_in, gain_one).astype(jnp.bfloat16)
    qkv = dense(normed, mixer_w[:, :qkv_width]).astype(jnp.bfloat16)
    outgate = dense(normed, mixer_w[:, qkv_width:wide])
    rank_rows = dense(normed, lowrank_w).astype(jnp.bfloat16)
    gate_logit = dense(rank_rows, rank_up_w) + bias_full.astype(jnp.float32)
    log_decay = jax.nn.log_sigmoid(gate_logit) / normalizer

    lower = jnp.tril(jnp.ones((BLOCK, BLOCK), jnp.float32))
    cumul3 = jnp.einsum(
        "ij,bjk->bik", lower, log_decay.reshape(block_count, BLOCK, KD), precision=highest
    )
    stops = cumul3[:, -1]
    strict = jnp.tril(jnp.ones((block_count, block_count), jnp.float32), -1)
    ahead_of = jnp.dot(strict, stops, precision=highest)
    after = jnp.dot(strict.T, stops, precision=highest)
    cumul = cumul3.reshape(count_of_rows, KD)
    query_f = qkv[:, :KD].astype(jnp.float32)
    key_f = qkv[:, KD : 2 * KD].astype(jnp.float32)
    value_rows = qkv[:, 2 * KD :]
    has_start = slice_start < count_of_rows
    at = jnp.arange(count_of_rows, dtype=jnp.int32)[:, None]
    to_end = jnp.exp((stops + after)[:, None, :] - cumul3).reshape(count_of_rows, KD)
    counts = jnp.logical_or(jnp.logical_not(has_start), at >= slice_start)
    key_to_end = jnp.where(counts, key_f * to_end, 0.0)
    from_first = jnp.exp(ahead_of[:, None, :] + cumul3).reshape(count_of_rows, KD)
    query_first = jnp.where(at < slice_start, query_f * from_first, 0.0)
    carry_decay = jnp.where(has_start, 0.0, jnp.exp(jnp.sum(stops, axis=0)))

    def heads(rows_of, width):
        return rows_of.reshape(count_of_rows, HEAD_COUNT, width)

    local_end = jnp.einsum(
        "thv,thk->hvk",
        heads(value_rows.astype(jnp.float32), VALUE_WIDTH),
        heads(key_to_end, DK),
        precision=high,
    ).reshape(VD, DK)
    incoming, decays = exchange_with_decay(local_end, carry_decay)
    mixed_rows, saved, gated_rows = mix_forward(
        seq_start, qkv, cumul, incoming, outgate, head_one
    )
    middle = residual_in + dense(gated_rows, output_w)
    normed_ffn = rms_norm(middle, gain_two).astype(jnp.bfloat16)
    width = w_gate.shape[1]
    gate_w = gate_up_w[:, :width]
    up_w = gate_up_w[:, width:]
    gate_pre = dense(normed_ffn, gate_w)
    up_pre = dense(normed_ffn, up_w)
    hidden = swiglu(gate_pre, up_pre).astype(jnp.bfloat16)
    output = row_major((middle + dense(hidden, down_w)).astype(jnp.bfloat16))

    grad_out = out_grad.astype(jnp.float32)
    down_sum = Reduction((hidden, out_grad))
    grad_hidden = dense_back(out_grad, down_w)
    unused, pull_swiglu = jax.vjp(swiglu, gate_pre, up_pre)
    grad_gate_f, grad_up_f = pull_swiglu(grad_hidden)
    grad_both = jnp.concatenate(
        [grad_gate_f.astype(jnp.bfloat16), grad_up_f.astype(jnp.bfloat16)], axis=1
    )
    grad_both = tie(grad_both, [down_sum])
    grad_normed_ffn = row_major(dense_back(grad_both, gate_up_w))
    unused, pull_norm_two = jax.vjp(rms_norm, middle, gain_two)
    grad_middle_part, grad_gain_two = pull_norm_two(grad_normed_ffn)
    grad_middle = row_major(grad_out + grad_middle_part)
    grad_attn = grad_middle.astype(jnp.bfloat16)
    grad_attn, grad_middle = tie((grad_attn, grad_middle), [down_sum])
    ffn_sum = Reduction((normed_ffn, grad_both), (gated_rows, grad_attn))
    grad_gated = dense_back(grad_attn, output_w)
    mixed_gradient, grad_outgate, carry_grad, grad_head = gate_backward(
        mixed_rows, outgate, grad_gated, query_first, head_one
    )
    grad_head = grad_head[0]
    outgoing = exchange_back(carry_grad, decays)
    outgoing = tie(outgoing, [down_sum, ffn_sum])
    grad_qkv, grad_decay = mix_backward(
        seq_start, qkv, cumul, mixed_gradient, saved, outgoing
    )
    grad_qkv, grad_decay = tie((grad_qkv, grad_decay), [down_sum, ffn_sum])
    mixer_sum = Reduction((normed, grad_qkv), (normed, grad_outgate))
    grad_logit = (grad_decay * jax.nn.sigmoid(-gate_logit) / normalizer).astype(jnp.bfloat16)
    grad_bias = jnp.sum(grad_logit.astype(jnp.float32), axis=0)
    grad_rank_up = dense_left(rank_rows, grad_logit)
    grad_rank = dense_back(grad_logit, rank_up_w).astype(jnp.bfloat16)
    grad_mixer = jnp.concatenate(
        [grad_qkv, grad_outgate, jnp.pad(grad_rank, ((0, 0), (0, SIDE - rank)))], axis=1
    )
    grad_normed = row_major(dense_back(grad_mixer, mixer_w))

    grad_normed = tie(grad_normed, [mixer_sum, ffn_sum, down_sum])
    unused, pull_norm_one = jax.vjp(rms_norm, residual_in, gain_one)
    grad_input_part, grad_gain_one = pull_norm_one(grad_normed)
    grad_tokens = (grad_middle + grad_input_part).astype(jnp.bfloat16)
    grad_tokens, grad_gain_one = tie((grad_tokens, grad_gain_one), [mixer_sum, down_sum])
    side_terms = [
        grad_gain_one,
        grad_gain_two,
        grad_bias,
        grad_head,
        grad_rank_up,
        dense_left(grad_rank, normed),
    ]
    side_sums = reduce_side(side_terms)
    at_shard = lax.axis_index("shard")

    def own(vector):
        size = vector.shape[-1] // shards
        return lax.dynamic_slice_in_dim(vector, at_shard * size, size, vector.ndim - 1)

    ((query_key, sum_value), outgate_halves) = mixer_sum.finish()
    ((sum_gate, sum_up), output_halves) = ffn_sum.finish()
    (down_halves,) = down_sum.finish()
    return (
        output,
        grad_tokens,
        own(side_sums[0]),
        query_key[:, :KD],
        query_key[:, KD:],
        sum_value,
        jnp.concatenate(outgate_halves, axis=1),
        own(side_sums[5]).T,
        own(side_sums[4].T).T,
        own(side_sums[2]),
        own(side_sums[3]),
        jnp.concatenate(output_halves, axis=1),
        own(side_sums[1]),
        sum_gate,
        sum_up,
        jnp.concatenate(down_halves, axis=1),
    )


def solution(mesh):
    return jax.shard_map(
        per_device,
        mesh=mesh,
        in_specs=(
            P(("replica", "shard"), None),
            P(("replica", "shard")),
            P(("replica", "shard"), None),
            P("shard"),
            P("shard", None),
            P("shard", None),
            P("shard", None),
            P("shard", None),
            P("shard", None),
            P("shard", None),
            P("shard"),
            P("shard"),
            P("shard", None),
            P("shard"),
            P("shard", None),
            P("shard", None),
            P("shard", None),
        ),
        out_specs=(
            P(("replica", "shard"), None),
            P(("replica", "shard"), None),
            P("shard"),
            P("shard", None),
            P("shard", None),
            P("shard", None),
            P("shard", None),
            P("shard", None),
            P("shard", None),
            P("shard"),
            P("shard"),
            P("shard", None),
            P("shard"),
            P("shard", None),
            P("shard", None),
            P("shard", None),
        ),
        check_vma=False,
    )
```

```python
import functools

import jax
import jax.numpy as jnp
from jax import lax
from jax.experimental import pallas as pl
from jax.experimental.layout import Layout, with_layout_constraint
from jax.experimental.pallas import tpu as pltpu
from jax.sharding import PartitionSpec as P

HEAD_COUNT = 4
DK = 128
VALUE_WIDTH = 256
BLOCK = 64
KD = HEAD_COUNT * DK
VD = HEAD_COUNT * VALUE_WIDTH
EVERY = ("replica", "shard")
ROWS = ("shard", "replica")
SIDE = 128
TAIL = 8

epsilon = 1e-05
normalizer = 16.0
highest = lax.Precision.HIGHEST
high = lax.Precision.HIGH


def dense(left, right):
    return jnp.dot(left, right, preferred_element_type=jnp.float32)


def dense_back(grad_rows, weight):
    return lax.dot_general(
        grad_rows, weight, (((1,), (1,)), ((), ())), preferred_element_type=jnp.float32
    )


def dense_left(input_rows, grad_rows):
    return lax.dot_general(
        input_rows, grad_rows, (((0,), (0,)), ((), ())), preferred_element_type=jnp.float32
    )


def row_major(value):
    return with_layout_constraint(value, Layout((0, 1)))


def rms_norm(values, gain):
    return values * lax.rsqrt(jnp.mean(values * values, axis=-1, keepdims=True) + epsilon) * gain


def swiglu(gate_pre, up_pre):
    return jax.nn.silu(gate_pre) * up_pre


def halves(a):
    if a.dtype == jnp.bfloat16:
        return (a, None)
    top = a.astype(jnp.bfloat16)
    return (top, (a - top.astype(jnp.float32)).astype(jnp.bfloat16))


def product(left, right, dims):
    def one(a, b):
        return lax.dot_general(a, b, (dims, ((), ())), preferred_element_type=jnp.float32)

    total = one(left[0], right[0])
    if left[1] is not None:
        total = total + one(left[1], right[0])
    if right[1] is not None:
        total = total + one(left[0], right[1])
    return total


def exact(left, right):
    return lax.dot_general(
        left, right, (NT, ((), ())), precision=highest, preferred_element_type=jnp.float32
    )


NN = ((1,), (0,))
NT = ((1,), (1,))
TN = ((0,), (0,))


def causal_mask():
    rows = lax.broadcasted_iota(jnp.int32, (BLOCK, BLOCK), 0)
    cols = lax.broadcasted_iota(jnp.int32, (BLOCK, BLOCK), 1)
    return rows >= cols


def forward_kernel(
    start_ref,
    qkv_ref,
    cumul_ref,
    incoming_ref,
    outgate_ref,
    gain_ref,
    mixed_ref,
    saved_ref,
    gated_ref,
    state_ref,
):
    block = pl.program_id(0)

    @pl.when(block == 0)
    def _():
        state_ref[...] = incoming_ref[...].astype(jnp.float32)

    keep = jnp.where(block * BLOCK == start_ref[0], 0.0, 1.0)
    causal = causal_mask()
    for h in range(HEAD_COUNT):
        ks = slice(h * DK, (h + 1) * DK)
        vs = slice(h * VALUE_WIDTH, (h + 1) * VALUE_WIDTH)
        query = qkv_ref[:, ks].astype(jnp.float32)
        key = qkv_ref[:, KD + h * DK : KD + (h + 1) * DK].astype(jnp.float32)
        value = qkv_ref[:, 2 * KD + h * VALUE_WIDTH : 2 * KD + (h + 1) * VALUE_WIDTH]
        cumul = cumul_ref[:, ks]
        stop = cumul[BLOCK - 1 :, :]
        state = state_ref[vs, :] * keep
        saved_ref[0, vs, :] = state
        query_f = query * jnp.exp(cumul)
        key_f = key * jnp.exp(-cumul)
        query_dec = halves(query_f)
        key_end = halves(key * jnp.exp(stop - cumul))
        scores = jnp.where(causal, exact(query_f, key_f), 0.0)
        mixed = product(query_dec, halves(state), NT) + product(
            halves(scores), (value, None), NN
        )
        mixed_ref[:, vs] = mixed
        outgate = outgate_ref[:, vs]
        shaped = rms_norm(mixed, gain_ref[...])
        gated_ref[:, vs] = (shaped * (outgate * jax.nn.sigmoid(outgate))).astype(jnp.bfloat16)
        state_ref[vs, :] = state * jnp.exp(stop) + product((value, None), key_end, TN)


def backward_kernel(
    start_ref, qkv_ref, cumul_ref, grad_ref, saved_ref, outgoing_ref, gqkv_ref, gdecay_ref, back_ref
):
    step = pl.program_id(0)
    block = pl.num_programs(0) - 1 - step

    @pl.when(step == 0)
    def _():
        back_ref[...] = outgoing_ref[...].astype(jnp.float32)

    keep = jnp.where(block * BLOCK == start_ref[0], 0.0, 1.0)
    causal = causal_mask()
    suffix = jnp.where(
        lax.broadcasted_iota(jnp.int32, (BLOCK, BLOCK), 0)
        <= lax.broadcasted_iota(jnp.int32, (BLOCK, BLOCK), 1),
        1.0,
        0.0,
    )
    last = lax.broadcasted_iota(jnp.int32, (BLOCK, DK), 0) == BLOCK - 1
    for h in range(HEAD_COUNT):
        ks = slice(h * DK, (h + 1) * DK)
        ks2 = slice(KD + h * DK, KD + (h + 1) * DK)
        vs = slice(h * VALUE_WIDTH, (h + 1) * VALUE_WIDTH)
        vs2 = slice(2 * KD + h * VALUE_WIDTH, 2 * KD + (h + 1) * VALUE_WIDTH)
        query = qkv_ref[:, ks].astype(jnp.float32)
        key = qkv_ref[:, ks2].astype(jnp.float32)
        value = (qkv_ref[:, vs2], None)
        cumul = cumul_ref[:, ks]
        stop = cumul[BLOCK - 1 :, :]
        grow = jnp.exp(cumul)
        shrink = jnp.exp(-cumul)
        to_end = jnp.exp(stop - cumul)
        whole = jnp.exp(stop)
        query_f = query * grow
        key_f = key * shrink
        end_f = key * to_end
        query_dec = halves(query_f)
        key_dec = halves(key_f)
        key_end = halves(end_f)
        grad_f = grad_ref[:, vs]
        grad = halves(grad_f)
        rest = (grad_f - grad[0].astype(jnp.float32)) - grad[1].astype(jnp.float32)
        grad_value = product(grad, value, NT) + product(
            (rest.astype(jnp.bfloat16), None), value, NT
        )
        state_f = saved_ref[0, vs, :]
        back_f = back_ref[vs, :]
        state = halves(state_f)
        back = halves(back_f)
        scores = halves(jnp.where(causal, product(query_dec, key_dec, NT), 0.0))
        pull = halves(jnp.where(causal, grad_value, 0.0))
        g_query_dec = product(grad, state, NN) + product(pull, key_dec, NN)
        g_key_dec = product(pull, query_dec, TN)
        g_key_end = product(value, back, NN)
        g_value = product(scores, grad, TN) + product(key_end, back, NT)
        gqkv_ref[:, ks] = (g_query_dec * grow).astype(jnp.bfloat16)
        gqkv_ref[:, ks2] = (g_key_dec * shrink + g_key_end * to_end).astype(jnp.bfloat16)
        gqkv_ref[:, vs2] = g_value.astype(jnp.bfloat16)
        end_part = g_key_end * end_f
        at_stop = jnp.sum(end_part, axis=0, keepdims=True) + whole * jnp.sum(
            state_f * back_f, axis=0, keepdims=True
        )
        g_cumul = g_query_dec * query_f - g_key_dec * key_f - end_part
        g_cumul = g_cumul + jnp.where(last, at_stop, 0.0)
        gdecay_ref[:, ks] = lax.dot_general(
            suffix, g_cumul, (NN, ((), ())), precision=highest, preferred_element_type=jnp.float32
        )
        back_ref[vs, :] = (back_f * whole + product(grad, query_dec, TN)) * keep


def rows_spec(width, index):
    return pl.BlockSpec((BLOCK, width), index)


def mix_forward(start, qkv, cumul, incoming, outgate, head_gain):
    count = qkv.shape[0] // BLOCK
    place = lambda i, s: (i, 0)
    return pl.pallas_call(
        forward_kernel,
        grid_spec=pltpu.PrefetchScalarGridSpec(
            num_scalar_prefetch=1,
            grid=(count,),
            in_specs=[
                rows_spec(2 * KD + VD, place),
                rows_spec(KD, place),
                pl.BlockSpec((VD, DK), lambda i, s: (0, 0)),
                rows_spec(VD, place),
                pl.BlockSpec((1, VALUE_WIDTH), lambda i, s: (0, 0)),
            ],
            out_specs=[
                rows_spec(VD, place),
                pl.BlockSpec((1, VD, DK), lambda i, s: (i, 0, 0)),
                rows_spec(VD, place),
            ],
            scratch_shapes=[pltpu.VMEM((VD, DK), jnp.float32)],
        ),
        out_shape=[
            jax.ShapeDtypeStruct((count * BLOCK, VD), jnp.float32),
            jax.ShapeDtypeStruct((count, VD, DK), jnp.float32),
            jax.ShapeDtypeStruct((count * BLOCK, VD), jnp.bfloat16),
        ],
        name="mix_forward",
    )(start, qkv, cumul, incoming, outgate, head_gain[None, :])


def gate_kernel(
    mixed_ref, outgate_ref, grad_ref, query_ref, gain_ref, gmixed_ref, gout_ref, carry_ref, ghead_ref
):
    @pl.when(pl.program_id(0) == 0)
    def _():
        carry_ref[...] = jnp.zeros_like(carry_ref)
        ghead_ref[...] = jnp.zeros_like(ghead_ref)

    gain = gain_ref[...]
    for h in range(HEAD_COUNT):
        ks = slice(h * DK, (h + 1) * DK)
        vs = slice(h * VALUE_WIDTH, (h + 1) * VALUE_WIDTH)
        mixed = mixed_ref[:, vs]
        outgate = outgate_ref[:, vs]
        grad = grad_ref[:, vs]
        scale = lax.rsqrt(jnp.mean(mixed * mixed, axis=-1, keepdims=True) + epsilon)
        unit = mixed * scale
        sigmoid = jax.nn.sigmoid(outgate)
        grad_shaped = grad * (outgate * sigmoid)
        gout_ref[:, vs] = (
            grad * (unit * gain) * (sigmoid * (1.0 + outgate * (1.0 - sigmoid)))
        ).astype(jnp.bfloat16)
        ghead_ref[...] += jnp.sum(grad_shaped * unit, axis=0, keepdims=True)
        grad_unit = grad_shaped * gain
        gmixed = scale * (
            grad_unit - unit * jnp.mean(grad_unit * unit, axis=-1, keepdims=True)
        )
        gmixed_ref[:, vs] = gmixed
        carry_ref[vs, :] += product(halves(gmixed), halves(query_ref[:, ks]), TN)


def gate_backward(mixed, outgate, grad, query, head_gain):
    rows = mixed.shape[0]
    block = 2 * BLOCK
    place = lambda i: (i, 0)
    fixed = lambda i: (0, 0)
    wide = pl.BlockSpec((block, VD), place)
    return pl.pallas_call(
        gate_kernel,
        grid=(rows // block,),
        in_specs=[
            wide,
            wide,
            wide,
            pl.BlockSpec((block, KD), place),
            pl.BlockSpec((1, VALUE_WIDTH), fixed),
        ],
        out_specs=[
            wide,
            wide,
            pl.BlockSpec((VD, DK), fixed),
            pl.BlockSpec((1, VALUE_WIDTH), fixed),
        ],
        out_shape=[
            jax.ShapeDtypeStruct((rows, VD), jnp.float32),
            jax.ShapeDtypeStruct((rows, VD), jnp.bfloat16),
            jax.ShapeDtypeStruct((VD, DK), jnp.float32),
            jax.ShapeDtypeStruct((1, VALUE_WIDTH), jnp.float32),
        ],
        name="gate_backward",
    )(mixed, outgate, grad, query, head_gain[None, :])


def mix_backward(start, qkv, cumul, grad, saved, outgoing):
    count = qkv.shape[0] // BLOCK
    place = lambda i, s: (count - 1 - i, 0)
    return pl.pallas_call(
        backward_kernel,
        grid_spec=pltpu.PrefetchScalarGridSpec(
            num_scalar_prefetch=1,
            grid=(count,),
            in_specs=[
                rows_spec(2 * KD + VD, place),
                rows_spec(KD, place),
                rows_spec(VD, place),
                pl.BlockSpec((1, VD, DK), lambda i, s: (count - 1 - i, 0, 0)),
                pl.BlockSpec((VD, DK), lambda i, s: (0, 0)),
            ],
            out_specs=[
                rows_spec(2 * KD + VD, place),
                rows_spec(KD, place),
            ],
            scratch_shapes=[pltpu.VMEM((VD, DK), jnp.float32)],
        ),
        out_shape=[
            jax.ShapeDtypeStruct((count * BLOCK, 2 * KD + VD), jnp.bfloat16),
            jax.ShapeDtypeStruct((count * BLOCK, KD), jnp.float32),
        ],
        name="mix_backward",
    )(start, qkv, cumul, grad, saved, outgoing)


def chain(pieces, decays, reverse):
    count = pieces.shape[0]

    def kernel(pieces_ref, decays_ref, out_ref):
        def one(step, state):
            at = count - 1 - step if reverse else step
            out_ref[at] = state.astype(jnp.bfloat16)
            return decays_ref[at] * state + pieces_ref[at].astype(jnp.float32)

        lax.fori_loop(0, count, one, jnp.zeros(pieces.shape[1:], jnp.float32))

    return pl.pallas_call(
        kernel,
        out_shape=jax.ShapeDtypeStruct(pieces.shape, jnp.bfloat16),
        name="chain_back" if reverse else "chain",
    )(pieces, decays)


def device_count():
    return lax.axis_size("replica") * lax.axis_size("shard")


def exchange_with_decay(state, decay):
    count = device_count()
    rows = VD // count
    top = decay.astype(jnp.bfloat16)
    rest = decay - top.astype(jnp.float32)
    middle = rest.astype(jnp.bfloat16)
    low = (rest - middle.astype(jnp.float32)).astype(jnp.bfloat16)
    terms = jnp.stack([top, middle, low]).reshape(3, HEAD_COUNT, DK).transpose(1, 0, 2)
    terms = jnp.pad(terms, ((0, 0), (0, TAIL - 3), (0, 0)))
    terms = jnp.repeat(terms, count // HEAD_COUNT, axis=0)
    sent = jnp.concatenate([state.astype(jnp.bfloat16).reshape(count, rows, DK), terms], axis=1)
    got = lax.all_to_all(sent, EVERY, 0, 0)
    decays = jnp.sum(got[:, rows : rows + 3].astype(jnp.float32), axis=1, keepdims=True)
    folded = chain(got[:, :rows], decays, False)
    return lax.all_to_all(folded, EVERY, 0, 0).reshape(VD, DK), decays


def exchange_back(state, decays):
    count = device_count()
    pieces = lax.all_to_all(
        state.astype(jnp.bfloat16).reshape(count, VD // count, DK), EVERY, 0, 0
    )
    folded = chain(pieces, decays, True)
    return lax.all_to_all(folded, EVERY, 0, 0).reshape(VD, DK)


def fetch(shard):
    piece = shard.shape[0] // lax.axis_size("replica")
    mine = lax.dynamic_slice_in_dim(shard, lax.axis_index("replica") * piece, piece, 0)
    return lax.all_gather(mine, ROWS, axis=0, tiled=True)


MESH = pl.DeviceIdType.MESH


def gather_kernel(shards, parts, piece_ref, whole_ref, local_sem, send_sem, recv_sem):
    at_z = lax.axis_index("shard")
    at_p = lax.axis_index("replica")
    core, at_x, at_y = at_p % 2, (at_p // 2) % 2, at_p // 4
    rows, width = piece_ref.shape
    small = rows // 8
    by_core = at_p + 1 - 2 * core
    by_x = at_p + 2 - 4 * at_x
    by_y = at_p + 4 - 8 * at_y
    plans = []
    low = 0
    for turn in range(parts):
        size = width // 128 * (turn + 1) // parts * 128 - low
        if turn % 2 == 0:
            plans.append((low, size, core * 4 + at_y * 2 + at_x, (by_x, by_y, by_core)))
        else:
            plans.append((low, size, core * 4 + at_x * 2 + at_y, (by_y, by_x, by_core)))
        low += size

    barrier = pltpu.get_barrier_semaphore()
    for step in range(1, shards):
        pl.semaphore_signal(
            barrier, inc=1, device_id=(at_p, (at_z + step) % shards), device_id_type=MESH
        )
    for partner in (by_core, by_x, by_y):
        pl.semaphore_signal(barrier, inc=1, device_id=(partner, at_z), device_id_type=MESH)
    pl.semaphore_wait(barrier, shards + 2)

    def place(owner, half, block, count):
        start = pl.multiple_of(owner * rows + block * small, small)
        low, size = plans[half][:2]
        return whole_ref.at[pl.ds(start, count * small), pl.ds(low, size)]

    def copy(source, target, step, half, stage, device):
        return pltpu.make_async_remote_copy(
            src_ref=source,
            dst_ref=target,
            send_sem=send_sem.at[step - 1, half, stage],
            recv_sem=recv_sem.at[step - 1, half, stage],
            device_id=device,
            device_id_type=MESH,
        )

    def first(step, half):
        low, size, block, _ = plans[half]
        source = piece_ref.at[pl.ds(pl.multiple_of(block * small, small), small), pl.ds(low, size)]
        target = place(at_z, half, block, 1)
        return copy(source, target, step, half, 0, (at_p, (at_z + step) % shards))

    def own_block(half, stage):
        block = plans[half][2]
        return block - block % (1 << stage)

    def other_block(half, stage):
        block = own_block(half, stage)
        size = 1 << stage
        return block + size - 2 * size * ((block // size) % 2)

    def later(step, half, stage):
        owner = (at_z + shards - step) % shards
        region = place(owner, half, own_block(half, stage), 1 << stage)
        return copy(region, region, step, half, stage + 1, (plans[half][3][stage], at_z))

    def arrived(step, half, stage):
        owner = (at_z + shards - step) % shards
        if stage < 0:
            region = place(owner, half, plans[half][2], 1)
        else:
            region = place(owner, half, other_block(half, stage), 1 << stage)
        copy(region, region, step, half, stage + 1, (at_p, (at_z + 1) % shards)).wait_recv()

    order = [1, shards - 1] + list(range(2, shards - 1))
    for step in order:
        for half in range(parts):
            first(step, half).start()
    local = pltpu.make_async_copy(
        piece_ref, whole_ref.at[pl.ds(pl.multiple_of(at_z * rows, rows), rows), :], local_sem
    )
    local.start()
    units = [(step, half) for step in order for half in range(parts)]
    lag = 2 if parts == 2 else 4
    for front in range(len(units) + 2 * lag):
        for stage in range(3):
            turn = front - lag * stage
            if 0 <= turn < len(units):
                arrived(*units[turn], stage - 1)
                later(*units[turn], stage).start()
    for step in order:
        for half in range(parts):
            arrived(step, half, 2)
            first(step, half).wait_send()
            for stage in range(3):
                later(step, half, stage).wait_send()
    local.wait()


def gather_now(shard, parts):
    shards = lax.axis_size("shard")
    if lax.axis_size("replica") != 8 or shard.shape[0] % 128 != 0:
        return fetch(shard)
    rows, width = shard.shape
    return pl.pallas_call(
        functools.partial(gather_kernel, shards, parts),
        in_specs=[pl.BlockSpec(memory_space=pltpu.VMEM)],
        out_specs=pl.BlockSpec(memory_space=pl.ANY),
        out_shape=jax.ShapeDtypeStruct((shards * rows, width), jnp.bfloat16),
        scratch_shapes=[
            pltpu.SemaphoreType.DMA,
            pltpu.SemaphoreType.DMA((shards - 1, parts, 4)),
            pltpu.SemaphoreType.DMA((shards - 1, parts, 4)),
        ],
        compiler_params=pltpu.CompilerParams(collective_id=0, has_side_effects=True),
        name="gather_now",
    )(shard)


def add_low(left, right):
    return (left.astype(jnp.float32) + right.astype(jnp.float32)).astype(jnp.bfloat16)


def flip(value, bit):
    size = lax.axis_size("replica")
    return lax.ppermute(value, "replica", [(i, i ^ (1 << bit)) for i in range(size)])


def bit_of(bit):
    return (lax.axis_index("replica") >> bit) & 1


def row_bits():
    return list(range(1, lax.axis_size("replica").bit_length() - 1))


def pick(view, bits, bit, other):
    at = bit_of(bit)
    return lax.dynamic_index_in_dim(view, 1 - at if other else at, 1 + bits.index(bit))


def column_half(right, other):
    half = right.shape[1] // 2
    at = bit_of(0)
    return lax.dynamic_slice_in_dim(right, (1 - at if other else at) * half, half, 1)


def reduce_stages(pairs, cuts):
    shards = lax.axis_size("shard")
    bits = row_bits()
    got = yield tuple(
        flip(dense_left(left, column_half(right, True)).astype(jnp.bfloat16), 0)
        for left, right in pairs
    )
    total = jnp.concatenate(
        [
            add_low(dense_left(left, column_half(right, False)), came)
            for (left, right), came in zip(pairs, got)
        ],
        axis=1,
    )
    half = total.shape[1]
    total = total.reshape((shards,) + (2,) * len(bits) + (-1, half))
    first, second = total[: shards // 2], total[shards // 2 :]
    for bit_a, bit_b in zip(bits, bits[::-1]):
        got_a = flip(pick(first, bits, bit_a, True), bit_a)
        got_b = flip(pick(second, bits, bit_b, True), bit_b)
        first, second, got_a, got_b = yield (first, second, got_a, got_b)
        first = add_low(pick(first, bits, bit_a, False), got_a)
        second = add_low(pick(second, bits, bit_b, False), got_b)
    total = jnp.concatenate([first, second], axis=0).reshape(shards, -1, half)
    size = total.shape[1] // cuts
    done = ()
    for cut in range(cuts):
        turn = lax.all_to_all(total[:, cut * size : (cut + 1) * size], "shard", 0, 0)
        state = yield (turn, total) + done
        total, done = state[1], state[2:] + state[:1]
    part = jnp.concatenate(
        [jnp.sum(got.astype(jnp.float32), axis=0).astype(jnp.bfloat16) for got in done], axis=0
    )
    rows = part.shape[0]
    part = part.reshape((1,) * len(bits) + (rows, half))
    first, second = part[..., : rows // 2, :], part[..., rows // 2 :, :]
    for bit_a, bit_b in zip(bits, bits[::-1]):
        first, second, got_a, got_b = yield (
            first,
            second,
            flip(first, bit_a),
            flip(second, bit_b),
        )
        first = joined_pair(first, got_a, bit_a, bits.index(bit_a))
        second = joined_pair(second, got_b, bit_b, bits.index(bit_b))
    whole = jnp.concatenate([first, second], axis=len(bits)).reshape(-1, half)
    whole, got = yield (whole, flip(whole, 0))
    return whole, got


def joined_pair(mine, got, bit, axis):
    return jnp.where(
        bit_of(bit) == 0,
        jnp.concatenate([mine, got], axis),
        jnp.concatenate([got, mine], axis),
    )


class Reduction:
    def __init__(self, *pairs, cuts=1):
        self.stages = reduce_stages(pairs, cuts)
        self.widths = [right.shape[1] // 2 for _, right in pairs]
        self.state = next(self.stages)
        self.result = None

    def advance(self, state):
        try:
            self.state = self.stages.send(state)
        except StopIteration as stop:
            self.state, self.result = None, stop.value

    def finish(self):
        while self.state is not None:
            self.advance(self.state)
        whole, got = self.result
        first = bit_of(0) == 0
        parts = []
        at = 0
        for width in self.widths:
            mine, came = whole[:, at : at + width], got[:, at : at + width]
            parts.append((jnp.where(first, mine, came), jnp.where(first, came, mine)))
            at += width
        return parts


def tie(values, jobs, hold=False):
    jobs = [job for job in jobs if job.state is not None]
    tied = lax.optimization_barrier((values, [job.state for job in jobs]))
    for job, state in zip(jobs, tied[1]):
        if hold:
            job.state = state
        else:
            job.advance(state)
    return tied[0]


def reduce_side(terms):
    count = device_count()
    flat = [term.astype(jnp.bfloat16).reshape(-1, SIDE) for term in terms]
    used = sum(part.shape[0] for part in flat)
    per = -(-used // count)
    rows = jnp.pad(jnp.concatenate(flat, axis=0), ((0, count * per - used), (0, 0)))
    got = lax.all_to_all(rows.reshape(count, per, SIDE), EVERY, 0, 0)
    part = jnp.sum(got.astype(jnp.float32), axis=0).astype(jnp.bfloat16)
    spread = jnp.broadcast_to(part[None], (count, per, SIDE))
    total = lax.all_to_all(spread, EVERY, 0, 0).reshape(count * per, SIDE).astype(jnp.float32)
    sums = []
    at = 0
    for term, part in zip(terms, flat):
        sums.append(total[at : at + part.shape[0]].reshape(term.shape))
        at += part.shape[0]
    return sums


def column(vector, rows):
    return jnp.pad(vector, (0, rows - vector.shape[0]))[:, None]


def per_device(
    tokens,
    seq_start,
    out_grad,
    norm_gain,
    w_query,
    w_key,
    w_value,
    w_outgate,
    w_lowrank,
    w_rank_up,
    gate_bias,
    head_gain,
    w_output,
    ffn_gain,
    w_gate,
    w_up,
    w_down,
):
    shards = lax.axis_size("shard")
    rows = w_query.shape[0]
    rank = w_lowrank.shape[1]
    spread = w_rank_up.size // rows
    at_norm = rank
    at_ffn = rank + 1
    at_bias = rank + 2
    at_head = rank + 3
    at_up = rank + 4
    side = jnp.concatenate(
        [
            w_lowrank,
            norm_gain[:, None],
            ffn_gain[:, None],
            column(gate_bias, rows),
            column(head_gain, rows),
            w_rank_up.reshape(rows, spread),
            jnp.zeros((rows, SIDE - at_up - spread), jnp.bfloat16),
        ],
        axis=1,
    )
    early = gather_now(
        jnp.concatenate([w_query, w_key, w_value, w_outgate, side, w_output], axis=1), 4
    )
    split = early.shape[1] - w_output.shape[1]
    mixer_w = early[:, :split]
    output_w = early[:, split:]
    gate_shard, up_shard, down_shard = (w_gate, w_up, w_down)
    gate_up_w = fetch(jnp.concatenate([gate_shard, up_shard], axis=1))
    down_w = fetch(down_shard)

    qkv_width = 2 * KD + VD
    wide = qkv_width + VD
    side_w = mixer_w[:, wide:]
    lowrank_w = side_w[:, :rank]
    gain_one = side_w[:, at_norm].astype(jnp.float32)
    gain_two = side_w[:, at_ffn].astype(jnp.float32)
    bias_full = side_w[:, at_bias].reshape(shards, rows)[:, : gate_bias.shape[0]].reshape(-1)
    head_one = (
        side_w[:, at_head].reshape(shards, rows)[:, : head_gain.shape[0]].reshape(-1)
    ).astype(jnp.float32)
    rank_up_w = side_w[:, at_up : at_up + spread].reshape(rank, KD)

    residual_in = tokens.astype(jnp.float32)
    count_of_rows = residual_in.shape[0]
    block_count = count_of_rows // BLOCK
    slice_start = seq_start[0]
    normed = rms_norm(residual_in, gain_one).astype(jnp.bfloat16)
    qkv = dense(normed, mixer_w[:, :qkv_width]).astype(jnp.bfloat16)
    outgate = dense(normed, mixer_w[:, qkv_width:wide])
    rank_rows = dense(normed, lowrank_w).astype(jnp.bfloat16)
    gate_logit = dense(rank_rows, rank_up_w) + bias_full.astype(jnp.float32)
    log_decay = jax.nn.log_sigmoid(gate_logit) / normalizer

    lower = jnp.tril(jnp.ones((BLOCK, BLOCK), jnp.float32))
    cumul3 = jnp.einsum(
        "ij,bjk->bik", lower, log_decay.reshape(block_count, BLOCK, KD), precision=highest
    )
    stops = cumul3[:, -1]
    strict = jnp.tril(jnp.ones((block_count, block_count), jnp.float32), -1)
    ahead_of = jnp.dot(strict, stops, precision=highest)
    after = jnp.dot(strict.T, stops, precision=highest)
    cumul = cumul3.reshape(count_of_rows, KD)
    query_f = qkv[:, :KD].astype(jnp.float32)
    key_f = qkv[:, KD : 2 * KD].astype(jnp.float32)
    value_rows = qkv[:, 2 * KD :]
    has_start = slice_start < count_of_rows
    at = jnp.arange(count_of_rows, dtype=jnp.int32)[:, None]
    to_end = jnp.exp((stops + after)[:, None, :] - cumul3).reshape(count_of_rows, KD)
    counts = jnp.logical_or(jnp.logical_not(has_start), at >= slice_start)
    key_to_end = jnp.where(counts, key_f * to_end, 0.0)
    from_first = jnp.exp(ahead_of[:, None, :] + cumul3).reshape(count_of_rows, KD)
    query_first = jnp.where(at < slice_start, query_f * from_first, 0.0)
    carry_decay = jnp.where(has_start, 0.0, jnp.exp(jnp.sum(stops, axis=0)))

    def heads(rows_of, width):
        return rows_of.reshape(count_of_rows, HEAD_COUNT, width)

    local_end = jnp.einsum(
        "thv,thk->hvk",
        heads(value_rows.astype(jnp.float32), VALUE_WIDTH),
        heads(key_to_end, DK),
        precision=high,
    ).reshape(VD, DK)
    incoming, decays = exchange_with_decay(local_end, carry_decay)
    mixed_rows, saved, gated_rows = mix_forward(
        seq_start, qkv, cumul, incoming, outgate, head_one
    )
    middle = residual_in + dense(gated_rows, output_w)
    normed_ffn = rms_norm(middle, gain_two).astype(jnp.bfloat16)
    width = w_gate.shape[1]
    gate_w = gate_up_w[:, :width]
    up_w = gate_up_w[:, width:]
    gate_pre = dense(normed_ffn, gate_w)
    up_pre = dense(normed_ffn, up_w)
    hidden = swiglu(gate_pre, up_pre).astype(jnp.bfloat16)
    output = row_major((middle + dense(hidden, down_w)).astype(jnp.bfloat16))

    grad_out = out_grad.astype(jnp.float32)
    down_sum = Reduction((hidden, out_grad))
    grad_hidden = dense_back(out_grad, down_w)
    unused, pull_swiglu = jax.vjp(swiglu, gate_pre, up_pre)
    grad_gate_f, grad_up_f = pull_swiglu(grad_hidden)
    grad_both = jnp.concatenate(
        [grad_gate_f.astype(jnp.bfloat16), grad_up_f.astype(jnp.bfloat16)], axis=1
    )
    grad_both = tie(grad_both, [down_sum])
    grad_normed_ffn = row_major(dense_back(grad_both, gate_up_w))
    unused, pull_norm_two = jax.vjp(rms_norm, middle, gain_two)
    grad_middle_part, grad_gain_two = pull_norm_two(grad_normed_ffn)
    grad_middle = row_major(grad_out + grad_middle_part)
    grad_attn = grad_middle.astype(jnp.bfloat16)
    grad_attn, grad_middle = tie((grad_attn, grad_middle), [down_sum])
    ffn_sum = Reduction((normed_ffn, grad_both), (gated_rows, grad_attn), cuts=2)
    grad_gated = dense_back(grad_attn, output_w)
    mixed_gradient, grad_outgate, carry_grad, grad_head = gate_backward(
        mixed_rows, outgate, grad_gated, query_first, head_one
    )
    grad_head = grad_head[0]
    mixed_gradient, grad_outgate, carry_grad = tie(
        (mixed_gradient, grad_outgate, carry_grad), [ffn_sum], hold=True
    )
    outgoing = exchange_back(carry_grad, decays)
    outgoing = tie(outgoing, [down_sum, ffn_sum])
    grad_qkv, grad_decay = mix_backward(
        seq_start, qkv, cumul, mixed_gradient, saved, outgoing
    )
    grad_qkv, grad_decay = tie((grad_qkv, grad_decay), [down_sum, ffn_sum])
    mixer_sum = Reduction((normed, grad_qkv), (normed, grad_outgate))
    grad_logit = (grad_decay * jax.nn.sigmoid(-gate_logit) / normalizer).astype(jnp.bfloat16)
    grad_bias = jnp.sum(grad_logit.astype(jnp.float32), axis=0)
    grad_rank_up = dense_left(rank_rows, grad_logit)
    grad_rank = dense_back(grad_logit, rank_up_w).astype(jnp.bfloat16)
    grad_mixer = jnp.concatenate(
        [grad_qkv, grad_outgate, jnp.pad(grad_rank, ((0, 0), (0, SIDE - rank)))], axis=1
    )
    grad_normed = row_major(dense_back(grad_mixer, mixer_w))

    grad_normed = tie(grad_normed, [mixer_sum, ffn_sum, down_sum])
    unused, pull_norm_one = jax.vjp(rms_norm, residual_in, gain_one)
    grad_input_part, grad_gain_one = pull_norm_one(grad_normed)
    grad_tokens = (grad_middle + grad_input_part).astype(jnp.bfloat16)
    grad_tokens, grad_gain_one = tie(
        (grad_tokens, grad_gain_one), [mixer_sum, ffn_sum, down_sum]
    )
    grad_gain_one = tie(grad_gain_one, [mixer_sum, ffn_sum])
    grad_gain_one = tie(grad_gain_one, [mixer_sum])
    side_terms = [
        grad_gain_one,
        grad_gain_two,
        grad_bias,
        grad_head,
        grad_rank_up,
        dense_left(grad_rank, normed),
    ]
    side_sums = reduce_side(side_terms)
    at_shard = lax.axis_index("shard")

    def own(vector):
        size = vector.shape[-1] // shards
        return lax.dynamic_slice_in_dim(vector, at_shard * size, size, vector.ndim - 1)

    def final(part):
        return part.astype(jnp.float32)

    ((query_key, sum_value), outgate_halves) = mixer_sum.finish()
    ((sum_gate, sum_up), output_halves) = ffn_sum.finish()
    (down_halves,) = down_sum.finish()
    return (
        output,
        grad_tokens,
        own(side_sums[0]),
        final(query_key[:, :KD]),
        final(query_key[:, KD:]),
        final(sum_value),
        final(jnp.concatenate(outgate_halves, axis=1)),
        own(side_sums[5]).T,
        own(side_sums[4].T).T,
        own(side_sums[2]),
        own(side_sums[3]),
        final(jnp.concatenate(output_halves, axis=1)),
        own(side_sums[1]),
        final(sum_gate),
        final(sum_up),
        final(jnp.concatenate(down_halves, axis=1)),
    )


def solution(mesh):
    return jax.shard_map(
        per_device,
        mesh=mesh,
        in_specs=(
            P(("replica", "shard"), None),
            P(("replica", "shard")),
            P(("replica", "shard"), None),
            P("shard"),
            P("shard", None),
            P("shard", None),
            P("shard", None),
            P("shard", None),
            P("shard", None),
            P("shard", None),
            P("shard"),
            P("shard"),
            P("shard", None),
            P("shard"),
            P("shard", None),
            P("shard", None),
            P("shard", None),
        ),
        out_specs=(
            P(("replica", "shard"), None),
            P(("replica", "shard"), None),
            P("shard"),
            P("shard", None),
            P("shard", None),
            P("shard", None),
            P("shard", None),
            P("shard", None),
            P("shard", None),
            P("shard"),
            P("shard"),
            P("shard", None),
            P("shard"),
            P("shard", None),
            P("shard", None),
            P("shard", None),
        ),
        check_vma=False,
    )
```
